32 devices in a mesh: slab: 2 (over y), lat: 16 (over z, x, core).
Axes of the slice: x: 2, y: 2, z: 4, core: 2. Of those that a mesh axis runs over, the one named last changes fastest.
Arguments:
- coef: bfloat16 [384, 769, 256], P('lat', None, 'slab'), parts along dimension 2, may hold values from -0.375 to 0.375
- legendre: bfloat16 [384, 769, 360], P('lat'), may hold values from -0.21875 to 0.21875
- m_of_pair: int32 [384], replicated, may hold values from 0 to 383, each once
- row_of_slot: int32 [368], replicated, may hold values from -1 to 359, as said below
Outputs:
- grid_out: bfloat16 [368, 2, 128, 1440], P('lat', None, 'slab'), parts along dimension 2
- spectrum: float32 [768, 128], P('lat', 'slab'), parts along dimension 1
The draws below stay inside these ranges and needn't reach their ends.
There are 2 independent parts, one for each index of `slab`. The reference program is written for one: setup_inputs(seed, part) draws one part's arguments, and reference() takes and returns one part's arrays. A program takes and returns all parts, laid end to end along the dimension named above; an argument that names none is the same for every part. Nothing has to cross between parts.
Inputs may be any that keep to these rules, and one draw needn't show every extreme that they name: `m_of_pair`: each of 0 to 383 appears once. `row_of_slot`: each northern row 0 to 359 is held by exactly one slot; all other slots hold -1.
All inputs are finite; a program needn't handle non-finite values.
Results may differ from the reference program's by a relative error of at most 0.0056.
Values may be sent and summed in bfloat16 or wider, within the bound.
No kernel may reach another device: no remote copies, remote signals or barrier semaphores. Data moves between devices by JAX's collectives and lax.ppermute only.
A program may use at most 192 MiB of HBM per device.

```python
import math
import jax
import jax.numpy as jnp
from jax import lax

MW = 768
LATH = 360
NLON = 1440
FIELDS = 64
PAIRS = 384
SLOTS = 368


def draw_row_of_slot(key, part):
    shuffled = jax.random.permutation(jax.random.fold_in(key, 7), SLOTS)
    return jnp.where(shuffled < LATH, shuffled, -1).astype(jnp.int32)


def levels(stream_key, extent, cuts, low, high):
    loudness = 1.0
    for dim, parts in cuts:
        draws = jax.random.uniform(jax.random.fold_in(jax.random.fold_in(stream_key, 6), dim), (parts,), jnp.float32, low / len(cuts), high / len(cuts))
        loudness = loudness * jnp.repeat(jnp.exp(draws), extent[dim] // parts).reshape((-1,) + (1,) * (len(extent) - 1 - dim))
    return loudness


def noise(rng, dims, spread, limit, cuts=(), kind=jnp.bfloat16):
    factor_of = levels(rng, dims, cuts, -0.22, 0.18) if cuts else 1.0
    array = jax.random.normal(rng, dims, jnp.float32) * spread * factor_of
    return jnp.minimum(jnp.maximum(array, -limit), limit).astype(kind)


def setup_inputs(seed: int = 0, part: int = 0) -> dict:
    splits = jax.random.split(jax.random.key(seed), 5)
    own_keys = jax.random.split(jax.random.fold_in(splits[4], part), 5)
    coef = noise(own_keys[0], (PAIRS, MW + 1, 2 * FIELDS), (0.7 / MW ** 0.5), 0.375, ((0, 16),))
    legendre = noise(splits[1], (PAIRS, MW + 1, LATH), MW ** -0.5, 0.21875, ((0, 16),))
    m_of_pair = jax.random.permutation(splits[2], PAIRS).astype(jnp.int32)
    row_of_slot = draw_row_of_slot(jax.random.fold_in(splits[4], 71), part)
    return dict(coef=coef, legendre=legendre, m_of_pair=m_of_pair, row_of_slot=row_of_slot)


def per_pair(operands):
    legend, coeffs, mask_set = operands
    masked = coeffs.astype(jnp.float32)[:, None, :] * mask_set[:, :, None]
    products = jnp.einsum('kh,kxc->xhc', legend.astype(jnp.float32), masked)
    even_part = products[0::2]
    odd_part = products[1::2]
    return jnp.stack([even_part + odd_part, even_part - odd_part], axis=1).astype(jnp.bfloat16)


def reference(coef, legendre, m_of_pair, row_of_slot):
    position = jnp.arange(MW + 1, dtype=jnp.int32)
    low_m = m_of_pair.astype(jnp.int32)
    in_low = position[None, :] < (MW - low_m)[:, None]
    parity = jnp.where(in_low, position[None, :] % 2, (position[None, :] - (MW - low_m)[:, None]) % 2)
    is_even = parity == 0
    mask_set = jnp.stack([in_low & is_even, in_low & ~is_even, ~in_low & is_even, ~in_low & ~is_even], axis=2).astype(jnp.float32)
    fourier = lax.map(per_pair, (legendre, coef, mask_set))

    wave = jnp.stack([low_m, MW - 1 - low_m], axis=1)
    longitude = jnp.arange(NLON, dtype=jnp.int32)
    angles = ((wave[:, :, None] * longitude[None, None, :]) % NLON).astype(jnp.float32) * (2.0 * math.pi / NLON)
    weights = jnp.where(wave == 0, 1.0, 2.0).astype(jnp.float32)[:, :, None]
    cos_table = (weights * jnp.cos(angles)).astype(jnp.bfloat16)
    sin_table = (-weights * jnp.sin(angles)).astype(jnp.bfloat16)
    dft_table = jnp.stack([cos_table, sin_table], axis=2).astype(jnp.float32)

    def per_slot(row_index):
        safe_row = jnp.maximum(row_index, 0).astype(jnp.int32)
        fourier_row = lax.dynamic_index_in_dim(fourier, safe_row, axis=3, keepdims=False)
        fourier_row = fourier_row.astype(jnp.float32).reshape(PAIRS, 2, 2, 2, FIELDS)
        values = jnp.einsum('pserf,psrj->efj', fourier_row, dft_table)
        return jnp.where(row_index >= 0, values, 0.0).astype(jnp.bfloat16)

    grid_out = lax.map(per_slot, row_of_slot)

    squares = coef.astype(jnp.float32) ** 2
    power_sum = squares[:, :, :FIELDS] + squares[:, :, FIELDS:]
    degree = jnp.where(in_low, low_m[:, None] + position[None, :], position[None, :] - 1)
    weight_term = jnp.where(in_low & (low_m[:, None] == 0), 1.0, 2.0).astype(jnp.float32)
    weighted = power_sum * weight_term[:, :, None]
    summed = jax.ops.segment_sum(weighted.reshape(-1, FIELDS), degree.reshape(-1), num_segments=MW)
    degree_value = jnp.arange(MW).astype(jnp.float32)
    spectrum = summed * (MW / (2.0 * degree_value + 1.0))[:, None]
    return grid_out, spectrum
```

```python
import functools
import math

import jax
import jax.numpy as jnp
from jax import lax
from jax.experimental import pallas as pl
from jax.experimental.pallas import tpu as pltpu
from jax.sharding import PartitionSpec as P

NLON = 1440
GROUP = 8
LANES = 128


def legendre_kernel(low_ref, slot_ref, leg_ref, coef_ref, out_ref, pick_ref, leg32_ref, coef32_ref, rows_ref, *, length):
    group = pl.program_id(0)
    slots, heights = pick_ref.shape
    columns = coef_ref.shape[2]
    fields = columns // 2
    tiles = leg32_ref.shape[0]

    @pl.when(group == 0)
    def _():
        height = lax.broadcasted_iota(jnp.int32, (slots, heights), 1)
        pick_ref[...] = jnp.where(height == slot_ref[...], 1.0, 0.0).astype(jnp.bfloat16)

    for tile in range(tiles):
        start = tile * LANES
        width = min(LANES, heights - start)
        piece = leg_ref[:, :, start : start + width].astype(jnp.float32)
        leg32_ref[tile, :, :width] = piece.reshape(length * GROUP, width)
    coef32_ref[...] = coef_ref[...].astype(jnp.float32).reshape(coef32_ref.shape)
    position = lax.broadcasted_iota(jnp.int32, (1, length), 1)
    for member in range(GROUP):
        cut = length - 1 - low_ref[group * GROUP + member]
        pick_rows = pl.ds(member, length, stride=GROUP)
        leg = jnp.concatenate([leg32_ref[tile, pick_rows, :] for tile in range(tiles)], axis=1)
        leg = leg[:, :heights].astype(jnp.bfloat16)
        coef = jnp.transpose(coef32_ref[pick_rows, :])
        in_low = position < cut
        operand = []
        for segment in range(2):
            keep = in_low if segment == 0 else jnp.logical_not(in_low)
            parity = lax.rem(position if segment == 0 else position + cut, 2)
            north = jnp.where(keep, 1.0, 0.0)
            south = jnp.where(parity == 0, north, -north)
            for part in range(2):
                values = coef[part * fields : (part + 1) * fields]
                operand += [values * north, values * south]
        operand = jnp.concatenate(operand, axis=0).astype(jnp.bfloat16)
        fourier = jnp.dot(operand, leg, preferred_element_type=jnp.float32).astype(jnp.bfloat16)
        taken = lax.dot_general(
            pick_ref[...], fourier, (((1,), (1,)), ((), ())), preferred_element_type=jnp.float32
        )
        for kind in range(4):
            rows_ref[kind, pl.ds(member, slots, stride=GROUP), :] = taken[
                :, kind * columns : (kind + 1) * columns
            ]
    for kind in range(4):
        out_ref[:, kind] = rows_ref[kind].reshape(slots, GROUP, columns).astype(jnp.bfloat16)


def legendre_rows(low_m, row_of_slot, legendre, coef):
    length, pairs, heights = legendre.shape
    columns = coef.shape[2]
    slots = row_of_slot.shape[0]
    return pl.pallas_call(
        functools.partial(legendre_kernel, length=length),
        out_shape=jax.ShapeDtypeStruct((slots, 4, pairs, columns), jnp.bfloat16),
        grid_spec=pltpu.PrefetchScalarGridSpec(
            num_scalar_prefetch=1,
            grid=(pairs // GROUP,),
            in_specs=[
                pl.BlockSpec((slots, 1), lambda group, low: (0, 0)),
                pl.BlockSpec((length, GROUP, heights), lambda group, low: (0, group, 0)),
                pl.BlockSpec((length, GROUP, columns), lambda group, low: (0, group, 0)),
            ],
            out_specs=pl.BlockSpec((slots, 4, GROUP, columns), lambda group, low: (0, 0, group, 0)),
            scratch_shapes=[
                pltpu.VMEM((slots, heights), jnp.bfloat16),
                pltpu.VMEM((pl.cdiv(heights, LANES), length * GROUP, LANES), jnp.float32),
                pltpu.VMEM((length * GROUP, columns), jnp.float32),
                pltpu.VMEM((4, slots * GROUP, columns), jnp.float32),
            ],
        ),
        compiler_params=pltpu.CompilerParams(vmem_limit_bytes=56 << 20),
        cost_estimate=pl.CostEstimate(
            flops=2 * pairs * 4 * columns * heights * (length + slots),
            bytes_accessed=2 * (legendre.size + coef.size + slots * 4 * pairs * columns),
            transcendentals=0,
        ),
    )(low_m, row_of_slot[:, None], legendre, coef)


def legendre_rows_plain(low_m, row_of_slot, legendre, coef):
    length = legendre.shape[0]
    fields = coef.shape[2] // 2
    position = jnp.arange(length, dtype=jnp.int32)[:, None]
    cut = (length - 1 - low_m)[None, :]
    in_low = position < cut
    parity = jnp.where(in_low, position, position + cut) % 2
    sign = jnp.where(parity == 0, 1.0, -1.0).astype(jnp.bfloat16)[:, :, None]
    kinds = []
    for keep in (in_low, ~in_low):
        kept = jnp.where(keep[:, :, None], coef, jnp.zeros((), coef.dtype))
        for part in range(2):
            values = kept[:, :, part * fields : (part + 1) * fields]
            kinds.append(jnp.concatenate([values, values * sign], axis=2))
    fourier = jnp.einsum(
        "kph,kpqc->hqpc", legendre, jnp.stack(kinds, axis=2), preferred_element_type=jnp.float32
    ).astype(jnp.bfloat16)
    taken = jnp.take(fourier, jnp.maximum(row_of_slot, 0), axis=0)
    return jnp.where((row_of_slot >= 0)[:, None, None, None], taken, jnp.zeros((), taken.dtype))


def dft_kernel(rows_ref, table_ref, out_ref):
    for slot in range(out_ref.shape[0]):
        rows = rows_ref[:, slot].reshape(table_ref.shape[0], rows_ref.shape[3])
        values = lax.dot_general(
            rows, table_ref[...], (((0,), (0,)), ((), ())), preferred_element_type=jnp.float32
        )
        out_ref[slot] = values.astype(jnp.bfloat16).reshape(out_ref.shape[1:])


def dft_rows(rows, table, step=2):
    sources, slots, depth, columns = rows.shape
    out_block = (step, 2, columns // 2, table.shape[1])
    return pl.pallas_call(
        dft_kernel,
        out_shape=jax.ShapeDtypeStruct((slots,) + out_block[1:], jnp.bfloat16),
        grid=(pl.cdiv(slots, step),),
        in_specs=[
            pl.BlockSpec((sources, step, depth, columns), lambda block: (0, block, 0, 0)),
            pl.BlockSpec(table.shape, lambda block: (0, 0), pipeline_mode=pl.Buffered(1)),
        ],
        out_specs=pl.BlockSpec(out_block, lambda block: (block, 0, 0, 0)),
        compiler_params=pltpu.CompilerParams(vmem_limit_bytes=40 << 20),
        cost_estimate=pl.CostEstimate(
            flops=2 * slots * columns * table.size,
            bytes_accessed=2 * (rows.size + table.size + slots * columns * table.shape[1]),
            transcendentals=0,
        ),
    )(rows, table)


def dft_rows_plain(rows, table):
    sources, slots, depth, columns = rows.shape
    values = jnp.einsum(
        "dlkc,dkj->lcj", rows, table.reshape(sources, depth, -1), preferred_element_type=jnp.float32
    )
    return values.astype(jnp.bfloat16).reshape(slots, 2, columns // 2, -1)


def dft_table(m_of_pair, wave_count, pairs_dev):
    low = m_of_pair.reshape(-1, 1, pairs_dev)
    wave = jnp.concatenate([low, wave_count - 1 - low], axis=1)[..., None]
    longitude = jnp.arange(NLON, dtype=jnp.int32)
    angles = (wave * longitude % NLON).astype(jnp.float32) * (2.0 * math.pi / NLON)
    weights = jnp.where(wave == 0, 1.0, 2.0).astype(jnp.float32)
    table = jnp.stack([weights * jnp.cos(angles), -weights * jnp.sin(angles)], axis=2)
    return table.astype(jnp.bfloat16).reshape(-1, NLON)


def spectrum_terms(coef, low_m):
    pairs_dev, length, columns = coef.shape
    wave_count = length - 1
    fields = columns // 2
    squares = coef.astype(jnp.float32) ** 2
    power_sum = squares[:, :, :fields] + squares[:, :, fields:]
    padded = jnp.concatenate(
        [jnp.zeros((pairs_dev, wave_count, fields), jnp.float32), power_sum[:, :wave_count]], axis=1
    )
    shifted = jax.vmap(
        lambda values, offset: lax.dynamic_slice_in_dim(values, offset, wave_count, 0)
    )(padded, wave_count - low_m)
    degree = jnp.arange(wave_count, dtype=jnp.int32)
    high_keep = (degree[None, :] >= (wave_count - 1 - low_m)[:, None]).astype(jnp.float32)
    high_terms = power_sum[:, 1:] * high_keep[:, :, None]
    low_weight = jnp.where(low_m == 0, 1.0, 2.0).astype(jnp.float32)
    return jnp.sum(low_weight[:, None, None] * shifted + 2.0 * high_terms, axis=0)


def local(coef, legendre, m_of_pair, row_of_slot):
    pairs_dev, length, columns = coef.shape
    wave_count = length - 1
    device = lax.axis_index("lat")
    low_m = lax.dynamic_slice_in_dim(m_of_pair, device * pairs_dev, pairs_dev)
    aligned = pairs_dev % GROUP == 0 and (4 * pairs_dev) % 16 == 0
    head = legendre_rows if aligned else legendre_rows_plain
    outgoing = head(
        low_m, row_of_slot, jnp.transpose(legendre, (1, 0, 2)), jnp.transpose(coef, (1, 0, 2))
    )
    outgoing = outgoing.reshape(outgoing.shape[0], 4 * pairs_dev, columns)
    incoming = lax.all_to_all(outgoing, "lat", split_axis=0, concat_axis=0, tiled=True)
    sources = m_of_pair.shape[0] // pairs_dev
    shaped = incoming.reshape(sources, -1, 4 * pairs_dev, columns)
    table = dft_table(m_of_pair, wave_count, pairs_dev)
    grid_out = (dft_rows if aligned else dft_rows_plain)(shaped, table)
    summed = lax.psum_scatter(spectrum_terms(coef, low_m), "lat", scatter_dimension=0, tiled=True)
    local_degree = (
        device * summed.shape[0] + jnp.arange(summed.shape[0], dtype=jnp.int32)
    ).astype(jnp.float32)
    spectrum = summed * (wave_count / (2.0 * local_degree + 1.0))[:, None]
    return (grid_out, spectrum)


def solution(mesh):
    in_specs = (P("lat", None, "slab"), P("lat", None, None), P(), P())
    out_specs = (P("lat", None, "slab", None), P("lat", "slab"))
    return jax.shard_map(local, mesh=mesh, in_specs=in_specs, out_specs=out_specs, check_vma=False)
```

```python
import functools
import math

import jax
import jax.numpy as jnp
from jax import lax
from jax.experimental import pallas as pl
from jax.experimental.pallas import tpu as pltpu
from jax.sharding import PartitionSpec as P

NLON = 1440
GROUP = 8
LANES = 128


def legendre_kernel(
    wave_ref, slot_ref, leg_ref, coef_ref, out_ref, pick_ref, leg32_ref, coef32_ref, rows_ref, *, length, first, pairs_dev, unroll
):
    group = pl.program_id(0)
    base = lax.axis_index("lat") * pairs_dev + (first + group) * GROUP
    slots, heights = pick_ref.shape
    columns = coef_ref.shape[2]
    fields = columns // 2
    tiles = leg32_ref.shape[0]

    @pl.when(group == 0)
    def _():
        height = lax.broadcasted_iota(jnp.int32, (heights, slots), 0)
        pick_ref[...] = jnp.transpose(jnp.where(height == slot_ref[...], 1.0, 0.0)).astype(jnp.bfloat16)

    for tile in range(tiles):
        start = tile * LANES
        width = min(LANES, heights - start)
        piece = leg_ref[:, :, start : start + width].astype(jnp.float32)
        leg32_ref[tile, :, :width] = piece.reshape(length * GROUP, width)
    coef32_ref[...] = coef_ref[...].astype(jnp.float32).reshape(coef32_ref.shape)
    even = length - 1
    position = lax.broadcasted_iota(jnp.int32, (1, even), 1)

    def one_pair(member):
        low = wave_ref[base + member]
        cut = even - low
        pick_rows = pl.ds(member, even, stride=GROUP)
        leg = jnp.concatenate([leg32_ref[tile, pick_rows, :] for tile in range(tiles)], axis=1)
        leg = leg[:, :heights].astype(jnp.bfloat16)
        coef = jnp.transpose(coef32_ref[pick_rows, :]).astype(jnp.bfloat16)
        in_low = position < cut
        operand = []
        for segment in range(2):
            keep = in_low if segment == 0 else jnp.logical_not(in_low)
            parity = lax.rem(position if segment == 0 else position + cut, 2)
            north = jnp.where(keep, 1.0, 0.0)
            south = jnp.where(parity == 0, north, -north).astype(jnp.bfloat16)
            north = north.astype(jnp.bfloat16)
            for part in range(2):
                values = coef[part * fields : (part + 1) * fields]
                operand += [values * north, values * south]
        operand = jnp.concatenate(operand, axis=0)
        fourier = jnp.dot(operand, leg, preferred_element_type=jnp.float32)
        last_row = pl.ds(even * GROUP + member, 1)
        last_leg = jnp.concatenate([leg32_ref[tile, last_row, :] for tile in range(tiles)], axis=1)
        last_coef = jnp.transpose(coef32_ref[last_row, :])
        sign = jnp.where(lax.rem(low, 2) == 0, 1.0, -1.0)
        halves = [last_coef[:fields], last_coef[fields:]]
        last = jnp.concatenate([v for h in halves for v in (h, h * sign)], axis=0)
        high = fourier[2 * columns :] + last * last_leg[:, :heights]
        fourier = jnp.concatenate([fourier[: 2 * columns], high], axis=0).astype(jnp.bfloat16)
        taken = lax.dot_general(
            pick_ref[...], fourier, (((1,), (1,)), ((), ())), preferred_element_type=jnp.float32
        )
        for kind in range(4):
            rows_ref[kind, pl.ds(member, slots, stride=GROUP), :] = taken[
                :, kind * columns : (kind + 1) * columns
            ]

    @pl.loop(0, GROUP // unroll)
    def _(step):
        for turn in range(unroll):
            one_pair(step * unroll + turn)

    for kind in range(4):
        out_ref[:, kind] = rows_ref[kind].reshape(slots, GROUP, columns).astype(jnp.bfloat16)


def legendre_rows(m_of_pair, row_of_slot, legendre, coef, first, groups, unroll):
    length, pairs_dev, heights = legendre.shape
    columns = coef.shape[2]
    slots = row_of_slot.shape[0]
    pairs = groups * GROUP
    return pl.pallas_call(
        functools.partial(
            legendre_kernel, length=length, first=first, pairs_dev=pairs_dev, unroll=unroll
        ),
        out_shape=jax.ShapeDtypeStruct((slots, 4, pairs, columns), jnp.bfloat16),
        grid_spec=pltpu.PrefetchScalarGridSpec(
            num_scalar_prefetch=1,
            grid=(groups,),
            in_specs=[
                pl.BlockSpec((1, slots), lambda group, wave: (0, 0)),
                pl.BlockSpec((length, GROUP, heights), lambda group, wave: (0, first + group, 0)),
                pl.BlockSpec((length, GROUP, columns), lambda group, wave: (0, first + group, 0)),
            ],
            out_specs=pl.BlockSpec((slots, 4, GROUP, columns), lambda group, wave: (0, 0, group, 0)),
            scratch_shapes=[
                pltpu.VMEM((slots, heights), jnp.bfloat16),
                pltpu.VMEM((pl.cdiv(heights, LANES), length * GROUP, LANES), jnp.float32),
                pltpu.VMEM((length * GROUP, columns), jnp.float32),
                pltpu.VMEM((4, slots * GROUP, columns), jnp.float32),
            ],
        ),
        compiler_params=pltpu.CompilerParams(vmem_limit_bytes=56 << 20),
        cost_estimate=pl.CostEstimate(
            flops=2 * pairs * 4 * columns * heights * (length + slots),
            bytes_accessed=2 * pairs * (length * (heights + columns) + slots * 4 * columns),
            transcendentals=0,
        ),
    )(m_of_pair, row_of_slot[None, :], legendre, coef)


def legendre_rows_plain(low_m, row_of_slot, legendre, coef):
    length = legendre.shape[0]
    fields = coef.shape[2] // 2
    position = jnp.arange(length, dtype=jnp.int32)[:, None]
    cut = (length - 1 - low_m)[None, :]
    in_low = position < cut
    parity = jnp.where(in_low, position, position + cut) % 2
    sign = jnp.where(parity == 0, 1.0, -1.0).astype(jnp.bfloat16)[:, :, None]
    kinds = []
    for keep in (in_low, ~in_low):
        kept = jnp.where(keep[:, :, None], coef, jnp.zeros((), coef.dtype))
        for part in range(2):
            values = kept[:, :, part * fields : (part + 1) * fields]
            kinds.append(jnp.concatenate([values, values * sign], axis=2))
    fourier = jnp.einsum(
        "kph,kpqc->hqpc", legendre, jnp.stack(kinds, axis=2), preferred_element_type=jnp.float32
    ).astype(jnp.bfloat16)
    taken = jnp.take(fourier, jnp.maximum(row_of_slot, 0), axis=0)
    return jnp.where((row_of_slot >= 0)[:, None, None, None], taken, jnp.zeros((), taken.dtype))


def dft_kernel(*refs, total):
    rows_ref, table_ref, *added, out_ref = refs
    for slot in range(out_ref.shape[0]):
        rows = rows_ref[:, slot].reshape(table_ref.shape[0], rows_ref.shape[3])
        values = lax.dot_general(
            rows, table_ref[...], (((0,), (0,)), ((), ())), preferred_element_type=jnp.float32
        ).reshape(out_ref.shape[1:])
        if total:
            values = values + added[0][slot]
        out_ref[slot] = values.astype(out_ref.dtype)


def dft_rows(rows, table, begin, *added, step=2):
    sources, slots, depth, columns = rows.shape
    depth = depth * sources
    total = bool(added)
    out_block = (step, 2, columns // 2, table.shape[1])
    out_spec = pl.BlockSpec(out_block, lambda block: (block, 0, 0, 0))
    return pl.pallas_call(
        functools.partial(dft_kernel, total=total),
        out_shape=jax.ShapeDtypeStruct(
            (slots,) + out_block[1:], jnp.bfloat16 if total else jnp.float32
        ),
        grid=(pl.cdiv(slots, step),),
        in_specs=[
            pl.BlockSpec((sources, step) + rows.shape[2:], lambda block: (0, block, 0, 0)),
            pl.BlockSpec(
                (depth, table.shape[1]),
                lambda block: (begin // depth, 0),
                pipeline_mode=pl.Buffered(1),
            ),
        ]
        + [out_spec] * len(added),
        out_specs=out_spec,
        compiler_params=pltpu.CompilerParams(vmem_limit_bytes=58 << 20),
        cost_estimate=pl.CostEstimate(
            flops=2 * slots * columns * depth * table.shape[1],
            bytes_accessed=2 * rows.size + (2 * depth + 6 * slots * columns) * table.shape[1],
            transcendentals=0,
        ),
    )(rows, table, *added)


def dft_rows_plain(rows, table):
    sources, slots, depth, columns = rows.shape
    values = jnp.einsum(
        "dlkc,dkj->lcj", rows, table.reshape(sources, depth, -1), preferred_element_type=jnp.float32
    )
    return values.astype(jnp.bfloat16).reshape(slots, 2, columns // 2, -1)


def dft_table(m_of_pair, wave_count, pairs_dev, cuts):
    low = m_of_pair.reshape(-1, 1, 1, pairs_dev)
    wave = jnp.concatenate([low, wave_count - 1 - low], axis=1)
    wave = jnp.broadcast_to(wave, (wave.shape[0], 2, 2, pairs_dev))
    shift = jnp.broadcast_to(jnp.array([0, NLON // 4], jnp.int32)[:, None], wave.shape)
    order = lambda values: jnp.concatenate(
        [values[..., begin:end].reshape(-1) for begin, end in cuts]
    )[:, None]
    wave, shift = order(wave), order(shift)
    longitude = jnp.arange(NLON, dtype=jnp.int32)
    angles = ((wave * longitude + shift) % NLON).astype(jnp.float32) * (2.0 * math.pi / NLON)
    weights = jnp.where(wave == 0, 1.0, 2.0).astype(jnp.float32)
    return (weights * jnp.cos(angles)).astype(jnp.bfloat16)


def dft_table_plain(m_of_pair, wave_count, pairs_dev):
    low = m_of_pair.reshape(-1, 1, pairs_dev)
    wave = jnp.concatenate([low, wave_count - 1 - low], axis=1)[..., None]
    longitude = jnp.arange(NLON, dtype=jnp.int32)
    angles = (wave * longitude % NLON).astype(jnp.float32) * (2.0 * math.pi / NLON)
    weights = jnp.where(wave == 0, 1.0, 2.0).astype(jnp.float32)
    table = jnp.stack([weights * jnp.cos(angles), -weights * jnp.sin(angles)], axis=2)
    return table.astype(jnp.bfloat16).reshape(-1, NLON)


def spectrum_terms(coef, low_m):
    pairs_dev, length, columns = coef.shape
    wave_count = length - 1
    fields = columns // 2
    squares = coef.astype(jnp.float32) ** 2
    power_sum = squares[:, :, :fields] + squares[:, :, fields:]
    padded = jnp.concatenate(
        [jnp.zeros((pairs_dev, wave_count, fields), jnp.float32), power_sum[:, :wave_count]], axis=1
    )
    shifted = jax.vmap(
        lambda values, offset: lax.dynamic_slice_in_dim(values, offset, wave_count, 0)
    )(padded, wave_count - low_m)
    degree = jnp.arange(wave_count, dtype=jnp.int32)
    high_keep = (degree[None, :] >= (wave_count - 1 - low_m)[:, None]).astype(jnp.float32)
    high_terms = power_sum[:, 1:] * high_keep[:, :, None]
    low_weight = jnp.where(low_m == 0, 1.0, 2.0).astype(jnp.float32)
    return jnp.sum(low_weight[:, None, None] * shifted + 2.0 * high_terms, axis=0)


def spectrum_kernel(wave_ref, coef_ref, out_ref, coef32_ref, low_ref, high_ref, *, pairs_dev):
    group = pl.program_id(0)
    base = lax.axis_index("lat") * pairs_dev + group * GROUP
    length, _, columns = coef_ref.shape
    wave_count = length - 1

    @pl.when(group == 0)
    def _():
        low_ref[...] = jnp.zeros_like(low_ref)
        high_ref[...] = jnp.zeros_like(high_ref)

    coef32_ref[...] = coef_ref[...].astype(jnp.float32).reshape(coef32_ref.shape)
    position = lax.broadcasted_iota(jnp.int32, (length, columns), 0)

    @pl.loop(0, GROUP)
    def _(member):
        low = wave_ref[base + member]
        values = coef32_ref[pl.ds(member, length, stride=GROUP), :]
        power = values * values
        in_low = position < wave_count - low
        weight = jnp.where(low == 0, 1.0, 2.0)
        low_ref[pl.ds(low, length), :] += jnp.where(in_low, weight * power, 0.0)
        high_ref[...] += jnp.where(in_low, 0.0, 2.0 * power)

    @pl.when(group == pl.num_programs(0) - 1)
    def _():
        terms = low_ref[pl.ds(0, wave_count), :] + high_ref[pl.ds(1, wave_count), :]
        terms = terms + pltpu.roll(terms, columns // 2, 1)
        out_ref[...] = terms[:, : columns // 2]


def spectrum_sums(m_of_pair, coef):
    length, pairs_dev, columns = coef.shape
    spare = length + (m_of_pair.shape[0] + 7) // 8 * 8
    return pl.pallas_call(
        functools.partial(spectrum_kernel, pairs_dev=pairs_dev),
        out_shape=jax.ShapeDtypeStruct((length - 1, columns // 2), jnp.float32),
        grid_spec=pltpu.PrefetchScalarGridSpec(
            num_scalar_prefetch=1,
            grid=(pairs_dev // GROUP,),
            in_specs=[pl.BlockSpec((length, GROUP, columns), lambda group, wave: (0, group, 0))],
            out_specs=pl.BlockSpec((length - 1, columns // 2), lambda group, wave: (0, 0)),
            scratch_shapes=[
                pltpu.VMEM((length * GROUP, columns), jnp.float32),
                pltpu.VMEM((spare, columns), jnp.float32),
                pltpu.VMEM((length, columns), jnp.float32),
            ],
        ),
        compiler_params=pltpu.CompilerParams(vmem_limit_bytes=24 << 20),
        cost_estimate=pl.CostEstimate(
            flops=8 * coef.size, bytes_accessed=2 * coef.size, transcendentals=0
        ),
    )(m_of_pair, coef)


def scale_kernel(summed_ref, after_ref, out_ref, *, wave_count):
    rows = summed_ref.shape[0]
    first = lax.axis_index("lat") * rows
    degree = (first + lax.broadcasted_iota(jnp.int32, summed_ref.shape, 0)).astype(jnp.float32)
    out_ref[...] = summed_ref[...] * (wave_count / (2.0 * degree + 1.0))


def spectrum_scale(summed, after, wave_count):
    whole = pl.BlockSpec(summed.shape, lambda: (0, 0))
    return pl.pallas_call(
        functools.partial(scale_kernel, wave_count=wave_count),
        out_shape=jax.ShapeDtypeStruct(summed.shape, summed.dtype),
        in_specs=[whole, pl.BlockSpec(memory_space=pl.ANY)],
        out_specs=whole,
    )(summed, after)


def exchange(outgoing, sources):
    incoming = lax.all_to_all(
        outgoing.reshape(outgoing.shape[0], -1, outgoing.shape[3]), "lat", split_axis=0, concat_axis=0, tiled=True
    )
    return incoming.reshape((sources, -1) + incoming.shape[1:])


def local(coef, legendre, m_of_pair, row_of_slot):
    pairs_dev, length, columns = coef.shape
    wave_count = length - 1
    device = lax.axis_index("lat")
    sources = m_of_pair.shape[0] // pairs_dev
    low_m = lax.dynamic_slice_in_dim(m_of_pair, device * pairs_dev, pairs_dev)
    legend_rows = jnp.transpose(legendre, (1, 0, 2))
    coef_rows = jnp.transpose(coef, (1, 0, 2))
    if pairs_dev % GROUP == 0 and pairs_dev > GROUP:
        groups = pairs_dev // GROUP
        rest = pairs_dev - GROUP
        head = functools.partial(legendre_rows, m_of_pair, row_of_slot, legend_rows, coef_rows)
        first_in = exchange(head(groups - 1, 1, 4), sources)
        second_in = exchange(head(0, groups - 1, 2), sources)
        table = dft_table(m_of_pair, wave_count, pairs_dev, ((0, rest), (rest, pairs_dev)))
        partial = dft_rows(first_in, table, 4 * sources * rest)
        grid_out = dft_rows(second_in, table, 0, partial)
        coef_rows, _ = lax.optimization_barrier((coef_rows, first_in[0, 0, 0, 0]))
        terms = spectrum_sums(m_of_pair, coef_rows)
        summed = lax.psum_scatter(terms, "lat", scatter_dimension=0, tiled=True)
        spectrum = spectrum_scale(summed, partial, wave_count)
    else:
        outgoing = legendre_rows_plain(low_m, row_of_slot, legend_rows, coef_rows)
        table = dft_table_plain(m_of_pair, wave_count, pairs_dev)
        grid_out = dft_rows_plain(exchange(outgoing, sources), table)
        terms = spectrum_terms(coef, low_m)
        summed = lax.psum_scatter(terms, "lat", scatter_dimension=0, tiled=True)
        local_degree = (
            device * summed.shape[0] + jnp.arange(summed.shape[0], dtype=jnp.int32)
        ).astype(jnp.float32)
        spectrum = summed * (wave_count / (2.0 * local_degree + 1.0))[:, None]
    return (grid_out, spectrum)


def solution(mesh):
    in_specs = (P("lat", None, "slab"), P("lat", None, None), P(), P())
    out_specs = (P("lat", None, "slab", None), P("lat", "slab"))
    return jax.shard_map(local, mesh=mesh, in_specs=in_specs, out_specs=out_specs, check_vma=False)
```

```python
import functools
import math

import jax
import jax.numpy as jnp
from jax import lax
from jax.experimental import pallas as pl
from jax.experimental.pallas import tpu as pltpu
from jax.sharding import PartitionSpec as P

NLON = 1440
GROUP = 8
LANES = 128


def legendre_kernel(
    wave_ref, slot_ref, leg_ref, coef_ref, out_ref, pick_ref, leg32_ref, coef32_ref, rows_ref, *, length, first, pairs_dev, unroll
):
    group = pl.program_id(0)
    base = lax.axis_index("lat") * pairs_dev + (first + group) * GROUP
    slots, heights = pick_ref.shape
    columns = coef_ref.shape[2]
    fields = columns // 2
    tiles = leg32_ref.shape[0]

    @pl.when(group == 0)
    def _():
        height = lax.broadcasted_iota(jnp.int32, (heights, slots), 0)
        pick_ref[...] = jnp.transpose(jnp.where(height == slot_ref[...], 1.0, 0.0)).astype(jnp.bfloat16)

    for tile in range(tiles):
        start = tile * LANES
        width = min(LANES, heights - start)
        piece = leg_ref[:, :, start : start + width].astype(jnp.float32)
        leg32_ref[tile, :, :width] = piece.reshape(length * GROUP, width)
    coef32_ref[...] = coef_ref[...].astype(jnp.float32).reshape(coef32_ref.shape)
    even = length - 1
    position = lax.broadcasted_iota(jnp.int32, (1, even), 1)

    def one_pair(member):
        low = wave_ref[base + member]
        cut = even - low
        pick_rows = pl.ds(member, even, stride=GROUP)
        leg = jnp.concatenate([leg32_ref[tile, pick_rows, :] for tile in range(tiles)], axis=1)
        leg = leg[:, :heights].astype(jnp.bfloat16)
        coef = jnp.transpose(coef32_ref[pick_rows, :]).astype(jnp.bfloat16)
        in_low = position < cut
        operand = []
        for segment in range(2):
            keep = in_low if segment == 0 else jnp.logical_not(in_low)
            parity = lax.rem(position if segment == 0 else position + cut, 2)
            north = jnp.where(keep, 1.0, 0.0)
            south = jnp.where(parity == 0, north, -north).astype(jnp.bfloat16)
            north = north.astype(jnp.bfloat16)
            for part in range(2):
                values = coef[part * fields : (part + 1) * fields]
                operand += [values * north, values * south]
        operand = jnp.concatenate(operand, axis=0)
        fourier = jnp.dot(operand, leg, preferred_element_type=jnp.float32)
        last_row = pl.ds(even * GROUP + member, 1)
        last_leg = jnp.concatenate([leg32_ref[tile, last_row, :] for tile in range(tiles)], axis=1)
        last_coef = jnp.transpose(coef32_ref[last_row, :])
        sign = jnp.where(lax.rem(low, 2) == 0, 1.0, -1.0)
        halves = [last_coef[:fields], last_coef[fields:]]
        last = jnp.concatenate([v for h in halves for v in (h, h * sign)], axis=0)
        high = fourier[2 * columns :] + last * last_leg[:, :heights]
        fourier = jnp.concatenate([fourier[: 2 * columns], high], axis=0).astype(jnp.bfloat16)
        taken = lax.dot_general(
            pick_ref[...], fourier, (((1,), (1,)), ((), ())), preferred_element_type=jnp.float32
        )
        for kind in range(4):
            rows_ref[kind, pl.ds(member, slots, stride=GROUP), :] = taken[
                :, kind * columns : (kind + 1) * columns
            ]

    @pl.loop(0, GROUP // unroll)
    def _(step):
        for turn in range(unroll):
            one_pair(step * unroll + turn)

    for kind in range(4):
        out_ref[:, kind] = rows_ref[kind].reshape(slots, GROUP, columns).astype(jnp.bfloat16)


def legendre_rows(m_of_pair, row_of_slot, legendre, coef, first, groups, unroll):
    length, pairs_dev, heights = legendre.shape
    columns = coef.shape[2]
    slots = row_of_slot.shape[0]
    pairs = groups * GROUP
    return pl.pallas_call(
        functools.partial(
            legendre_kernel, length=length, first=first, pairs_dev=pairs_dev, unroll=unroll
        ),
        out_shape=jax.ShapeDtypeStruct((slots, 4, pairs, columns), jnp.bfloat16),
        grid_spec=pltpu.PrefetchScalarGridSpec(
            num_scalar_prefetch=1,
            grid=(groups,),
            in_specs=[
                pl.BlockSpec((1, slots), lambda group, wave: (0, 0)),
                pl.BlockSpec((length, GROUP, heights), lambda group, wave: (0, first + group, 0)),
                pl.BlockSpec((length, GROUP, columns), lambda group, wave: (0, first + group, 0)),
            ],
            out_specs=pl.BlockSpec((slots, 4, GROUP, columns), lambda group, wave: (0, 0, group, 0)),
            scratch_shapes=[
                pltpu.VMEM((slots, heights), jnp.bfloat16),
                pltpu.VMEM((pl.cdiv(heights, LANES), length * GROUP, LANES), jnp.float32),
                pltpu.VMEM((length * GROUP, columns), jnp.float32),
                pltpu.VMEM((4, slots * GROUP, columns), jnp.float32),
            ],
        ),
        compiler_params=pltpu.CompilerParams(vmem_limit_bytes=56 << 20),
        cost_estimate=pl.CostEstimate(
            flops=2 * pairs * 4 * columns * heights * (length + slots),
            bytes_accessed=2 * pairs * (length * (heights + columns) + slots * 4 * columns),
            transcendentals=0,
        ),
    )(m_of_pair, row_of_slot[None, :], legendre, coef)


def legendre_rows_plain(low_m, row_of_slot, legendre, coef):
    length = legendre.shape[0]
    fields = coef.shape[2] // 2
    position = jnp.arange(length, dtype=jnp.int32)[:, None]
    cut = (length - 1 - low_m)[None, :]
    in_low = position < cut
    parity = jnp.where(in_low, position, position + cut) % 2
    sign = jnp.where(parity == 0, 1.0, -1.0).astype(jnp.bfloat16)[:, :, None]
    kinds = []
    for keep in (in_low, ~in_low):
        kept = jnp.where(keep[:, :, None], coef, jnp.zeros((), coef.dtype))
        for part in range(2):
            values = kept[:, :, part * fields : (part + 1) * fields]
            kinds.append(jnp.concatenate([values, values * sign], axis=2))
    fourier = jnp.einsum(
        "kph,kpqc->hqpc", legendre, jnp.stack(kinds, axis=2), preferred_element_type=jnp.float32
    ).astype(jnp.bfloat16)
    taken = jnp.take(fourier, jnp.maximum(row_of_slot, 0), axis=0)
    return jnp.where((row_of_slot >= 0)[:, None, None, None], taken, jnp.zeros((), taken.dtype))


def dft_kernel(*refs, total):
    rows_ref, table_ref, *added, out_ref = refs
    for slot in range(out_ref.shape[0]):
        rows = rows_ref[:, slot].reshape(table_ref.shape[0], rows_ref.shape[3])
        values = lax.dot_general(
            rows, table_ref[...], (((0,), (0,)), ((), ())), preferred_element_type=jnp.float32
        ).reshape(out_ref.shape[1:])
        if total:
            values = values + added[0][slot]
        out_ref[slot] = values.astype(out_ref.dtype)


def dft_rows(rows, table, begin, *added, step=4):
    sources, slots, depth, columns = rows.shape
    depth = depth * sources
    total = bool(added)
    out_block = (step, 2, columns // 2, table.shape[1])
    out_spec = pl.BlockSpec(out_block, lambda block: (block, 0, 0, 0))
    return pl.pallas_call(
        functools.partial(dft_kernel, total=total),
        out_shape=jax.ShapeDtypeStruct(
            (slots,) + out_block[1:], jnp.bfloat16 if total else jnp.float32
        ),
        grid=(pl.cdiv(slots, step),),
        in_specs=[
            pl.BlockSpec((sources, step) + rows.shape[2:], lambda block: (0, block, 0, 0)),
            pl.BlockSpec(
                (depth, table.shape[1]),
                lambda block: (begin // depth, 0),
                pipeline_mode=pl.Buffered(1),
            ),
        ]
        + [out_spec] * len(added),
        out_specs=out_spec,
        compiler_params=pltpu.CompilerParams(vmem_limit_bytes=58 << 20),
        cost_estimate=pl.CostEstimate(
            flops=2 * slots * columns * depth * table.shape[1],
            bytes_accessed=2 * rows.size + (2 * depth + 6 * slots * columns) * table.shape[1],
            transcendentals=0,
        ),
    )(rows, table, *added)


def dft_rows_plain(rows, table):
    sources, slots, depth, columns = rows.shape
    values = jnp.einsum(
        "dlkc,dkj->lcj", rows, table.reshape(sources, depth, -1), preferred_element_type=jnp.float32
    )
    return values.astype(jnp.bfloat16).reshape(slots, 2, columns // 2, -1)


def dft_table(m_of_pair, wave_count, pairs_dev, cuts):
    low = m_of_pair.reshape(-1, 1, 1, pairs_dev)
    wave = jnp.concatenate([low, wave_count - 1 - low], axis=1)
    wave = jnp.broadcast_to(wave, (wave.shape[0], 2, 2, pairs_dev))
    shift = jnp.broadcast_to(jnp.array([0, NLON // 4], jnp.int32)[:, None], wave.shape)
    order = lambda values: jnp.concatenate(
        [values[..., begin:end].reshape(-1) for begin, end in cuts]
    )[:, None]
    wave, shift = order(wave), order(shift)
    longitude = jnp.arange(NLON, dtype=jnp.int32)
    angles = ((wave * longitude + shift) % NLON).astype(jnp.float32) * (2.0 * math.pi / NLON)
    weights = jnp.where(wave == 0, 1.0, 2.0).astype(jnp.float32)
    return (weights * jnp.cos(angles)).astype(jnp.bfloat16)


def dft_table_plain(m_of_pair, wave_count, pairs_dev):
    low = m_of_pair.reshape(-1, 1, pairs_dev)
    wave = jnp.concatenate([low, wave_count - 1 - low], axis=1)[..., None]
    longitude = jnp.arange(NLON, dtype=jnp.int32)
    angles = (wave * longitude % NLON).astype(jnp.float32) * (2.0 * math.pi / NLON)
    weights = jnp.where(wave == 0, 1.0, 2.0).astype(jnp.float32)
    table = jnp.stack([weights * jnp.cos(angles), -weights * jnp.sin(angles)], axis=2)
    return table.astype(jnp.bfloat16).reshape(-1, NLON)


def spectrum_terms(coef, low_m):
    pairs_dev, length, columns = coef.shape
    wave_count = length - 1
    fields = columns // 2
    squares = coef.astype(jnp.float32) ** 2
    power_sum = squares[:, :, :fields] + squares[:, :, fields:]
    padded = jnp.concatenate(
        [jnp.zeros((pairs_dev, wave_count, fields), jnp.float32), power_sum[:, :wave_count]], axis=1
    )
    shifted = jax.vmap(
        lambda values, offset: lax.dynamic_slice_in_dim(values, offset, wave_count, 0)
    )(padded, wave_count - low_m)
    degree = jnp.arange(wave_count, dtype=jnp.int32)
    high_keep = (degree[None, :] >= (wave_count - 1 - low_m)[:, None]).astype(jnp.float32)
    high_terms = power_sum[:, 1:] * high_keep[:, :, None]
    low_weight = jnp.where(low_m == 0, 1.0, 2.0).astype(jnp.float32)
    return jnp.sum(low_weight[:, None, None] * shifted + 2.0 * high_terms, axis=0)


def spectrum_kernel(wave_ref, coef_ref, after_ref, out_ref, coef32_ref, low_ref, high_ref, *, pairs_dev):
    group = pl.program_id(0)
    base = lax.axis_index("lat") * pairs_dev + group * GROUP
    length, _, columns = coef_ref.shape
    wave_count = length - 1

    @pl.when(group == 0)
    def _():
        low_ref[...] = jnp.zeros_like(low_ref)
        high_ref[...] = jnp.zeros_like(high_ref)

    coef32_ref[...] = coef_ref[...].astype(jnp.float32).reshape(coef32_ref.shape)
    position = lax.broadcasted_iota(jnp.int32, (length, columns), 0)

    @pl.loop(0, GROUP)
    def _(member):
        low = wave_ref[base + member]
        values = coef32_ref[pl.ds(member, length, stride=GROUP), :]
        power = values * values
        in_low = position < wave_count - low
        weight = jnp.where(low == 0, 1.0, 2.0)
        low_ref[pl.ds(low, length), :] += jnp.where(in_low, weight * power, 0.0)
        high_ref[...] += jnp.where(in_low, 0.0, 2.0 * power)

    @pl.when(group == pl.num_programs(0) - 1)
    def _():
        terms = low_ref[pl.ds(0, wave_count), :] + high_ref[pl.ds(1, wave_count), :]
        terms = terms + pltpu.roll(terms, columns // 2, 1)
        out_ref[...] = terms[:, : columns // 2]


def spectrum_sums(m_of_pair, coef, after):
    length, pairs_dev, columns = coef.shape
    spare = length + (m_of_pair.shape[0] + 7) // 8 * 8
    return pl.pallas_call(
        functools.partial(spectrum_kernel, pairs_dev=pairs_dev),
        out_shape=jax.ShapeDtypeStruct((length - 1, columns // 2), jnp.float32),
        grid_spec=pltpu.PrefetchScalarGridSpec(
            num_scalar_prefetch=1,
            grid=(pairs_dev // GROUP,),
            in_specs=[
                pl.BlockSpec((length, GROUP, columns), lambda group, wave: (0, group, 0)),
                pl.BlockSpec(memory_space=pl.ANY),
            ],
            out_specs=pl.BlockSpec((length - 1, columns // 2), lambda group, wave: (0, 0)),
            scratch_shapes=[
                pltpu.VMEM((length * GROUP, columns), jnp.float32),
                pltpu.VMEM((spare, columns), jnp.float32),
                pltpu.VMEM((length, columns), jnp.float32),
            ],
        ),
        compiler_params=pltpu.CompilerParams(vmem_limit_bytes=58 << 20),
        cost_estimate=pl.CostEstimate(
            flops=8 * coef.size, bytes_accessed=2 * coef.size, transcendentals=0
        ),
    )(m_of_pair, coef, after)


def sum_kernel(own_ref, *refs, scale):
    *got, _, out_ref = refs
    summed = own_ref[...]
    for piece in got:
        summed = summed + piece[...]
    if scale:
        first = lax.axis_index("lat") * own_ref.shape[0]
        degree = (first + lax.broadcasted_iota(jnp.int32, own_ref.shape, 0)).astype(jnp.float32)
        summed = summed * (scale / (2.0 * degree + 1.0))
    out_ref[...] = summed


def sum_pieces(pieces, after, scale=0):
    shape = pieces[0].shape
    whole = pl.BlockSpec(shape, lambda: (0, 0))
    return pl.pallas_call(
        functools.partial(sum_kernel, scale=scale),
        out_shape=jax.ShapeDtypeStruct(shape, pieces[0].dtype),
        in_specs=[whole] * len(pieces) + [pl.BlockSpec(memory_space=pl.ANY)],
        out_specs=whole,
        compiler_params=pltpu.CompilerParams(vmem_limit_bytes=58 << 20),
    )(*pieces, after)


def gate_kernel(*refs):
    pass


def gate(value, *others):
    anywhere = pl.BlockSpec(memory_space=pl.ANY)
    return pl.pallas_call(
        gate_kernel,
        out_shape=jax.ShapeDtypeStruct(value.shape, value.dtype),
        in_specs=[anywhere] * (1 + len(others)),
        out_specs=anywhere,
        input_output_aliases={0: 0},
        compiler_params=pltpu.CompilerParams(vmem_limit_bytes=58 << 20),
    )(value, *others)


def scatter_round(terms, sources, stride, members):
    index = lax.axis_index("lat") // stride % members
    blocks = terms.reshape((members, -1) + terms.shape[1:])
    mine = lambda step: lax.dynamic_index_in_dim(blocks, index ^ step, 0, keepdims=False)
    pieces = [mine(0)]
    for step in range(1, members):
        pairs = [(i, i ^ (step * stride)) for i in range(sources)]
        pieces.append(lax.ppermute(mine(step), "lat", pairs))
    return pieces


def exchange(outgoing, sources):
    incoming = lax.all_to_all(
        outgoing.reshape(outgoing.shape[0], -1, outgoing.shape[3]), "lat", split_axis=0, concat_axis=0, tiled=True
    )
    return incoming.reshape((sources, -1) + incoming.shape[1:])


def local(coef, legendre, m_of_pair, row_of_slot):
    pairs_dev, length, columns = coef.shape
    wave_count = length - 1
    device = lax.axis_index("lat")
    sources = m_of_pair.shape[0] // pairs_dev
    low_m = lax.dynamic_slice_in_dim(m_of_pair, device * pairs_dev, pairs_dev)
    legend_rows = jnp.transpose(legendre, (1, 0, 2))
    coef_rows = jnp.transpose(coef, (1, 0, 2))
    if pairs_dev % GROUP == 0 and pairs_dev > GROUP and sources == 16:
        groups = pairs_dev // GROUP
        rest = pairs_dev - GROUP
        head = functools.partial(legendre_rows, m_of_pair, row_of_slot, legend_rows, coef_rows)
        outgoing = head(groups - 1, 1, 4)
        first_in = exchange(outgoing, sources)
        terms = spectrum_sums(m_of_pair, coef_rows, outgoing)
        pieces = scatter_round(terms, sources, 4, sources // 4)
        second_in = exchange(gate(head(0, groups - 1, 2), *pieces[1:]), sources)
        table = dft_table(m_of_pair, wave_count, pairs_dev, ((0, rest), (rest, pairs_dev)))
        partial = dft_rows(first_in, table, 4 * sources * rest)
        grid_out = dft_rows(second_in, table, 0, partial)
        pieces = scatter_round(sum_pieces(pieces, partial), sources, 1, 4)
        spectrum = sum_pieces(pieces, grid_out, wave_count)
    else:
        outgoing = legendre_rows_plain(low_m, row_of_slot, legend_rows, coef_rows)
        table = dft_table_plain(m_of_pair, wave_count, pairs_dev)
        grid_out = dft_rows_plain(exchange(outgoing, sources), table)
        terms = spectrum_terms(coef, low_m)
        summed = lax.psum_scatter(terms, "lat", scatter_dimension=0, tiled=True)
        local_degree = (
            device * summed.shape[0] + jnp.arange(summed.shape[0], dtype=jnp.int32)
        ).astype(jnp.float32)
        spectrum = summed * (wave_count / (2.0 * local_degree + 1.0))[:, None]
    return (grid_out, spectrum)


def solution(mesh):
    in_specs = (P("lat", None, "slab"), P("lat", None, None), P(), P())
    out_specs = (P("lat", None, "slab", None), P("lat", "slab"))
    return jax.shard_map(local, mesh=mesh, in_specs=in_specs, out_specs=out_specs, check_vma=False)
```

```python
import functools
import math

import jax
import jax.numpy as jnp
from jax import lax
from jax.experimental import pallas as pl
from jax.experimental.pallas import tpu as pltpu
from jax.sharding import PartitionSpec as P

NLON = 1440
GROUP = 8
LANES = 128


def legendre_kernel(
    wave_ref, slot_ref, leg_ref, coef_ref, out_ref, pick_ref, leg32_ref, coef32_ref, rows_ref, *, length, first, pairs_dev, unroll
):
    group = pl.program_id(0)
    base = lax.axis_index("lat") * pairs_dev + (first + group) * GROUP
    slots, heights = pick_ref.shape
    columns = coef_ref.shape[2]
    fields = columns // 2
    tiles = leg32_ref.shape[0]

    @pl.when(group == 0)
    def _():
        height = lax.broadcasted_iota(jnp.int32, (heights, slots), 0)
        pick_ref[...] = jnp.transpose(jnp.where(height == slot_ref[...].reshape(1, slots), 1.0, 0.0)).astype(jnp.bfloat16)

    for tile in range(tiles):
        start = tile * LANES
        width = min(LANES, heights - start)
        piece = leg_ref[:, :, start : start + width].astype(jnp.float32)
        leg32_ref[tile, :, :width] = piece.reshape(length * GROUP, width)
    coef32_ref[...] = coef_ref[...].astype(jnp.float32).reshape(coef32_ref.shape)
    even = length - 1
    position = lax.broadcasted_iota(jnp.int32, (1, even), 1)

    def one_pair(member):
        low = wave_ref[base + member]
        cut = even - low
        pick_rows = pl.ds(member, even, stride=GROUP)
        leg = jnp.concatenate([leg32_ref[tile, pick_rows, :] for tile in range(tiles)], axis=1)
        leg = leg[:, :heights].astype(jnp.bfloat16)
        coef = jnp.transpose(coef32_ref[pick_rows, :]).astype(jnp.bfloat16)
        in_low = position < cut
        operand = []
        for segment in range(2):
            keep = in_low if segment == 0 else jnp.logical_not(in_low)
            parity = lax.rem(position if segment == 0 else position + cut, 2)
            north = jnp.where(keep, 1.0, 0.0)
            south = jnp.where(parity == 0, north, -north).astype(jnp.bfloat16)
            north = north.astype(jnp.bfloat16)
            for part in range(2):
                values = coef[part * fields : (part + 1) * fields]
                operand += [values * north, values * south]
        operand = jnp.concatenate(operand, axis=0)
        fourier = jnp.dot(operand, leg, preferred_element_type=jnp.float32)
        last_row = pl.ds(even * GROUP + member, 1)
        last_leg = jnp.concatenate([leg32_ref[tile, last_row, :] for tile in range(tiles)], axis=1)
        last_coef = jnp.transpose(coef32_ref[last_row, :])
        sign = jnp.where(lax.rem(low, 2) == 0, 1.0, -1.0)
        halves = [last_coef[:fields], last_coef[fields:]]
        last = jnp.concatenate([v for h in halves for v in (h, h * sign)], axis=0)
        high = fourier[2 * columns :] + last * last_leg[:, :heights]
        fourier = jnp.concatenate([fourier[: 2 * columns], high], axis=0).astype(jnp.bfloat16)
        taken = lax.dot_general(
            pick_ref[...], fourier, (((1,), (1,)), ((), ())), preferred_element_type=jnp.float32
        )
        for kind in range(4):
            rows_ref[kind, pl.ds(member, slots, stride=GROUP), :] = taken[
                :, kind * columns : (kind + 1) * columns
            ]

    @pl.loop(0, GROUP // unroll)
    def _(step):
        for turn in range(unroll):
            one_pair(step * unroll + turn)

    for kind in range(4):
        out_ref[:, kind] = rows_ref[kind].reshape(slots, GROUP, columns).astype(jnp.bfloat16)


def legendre_rows(m_of_pair, row_of_slot, legendre, coef, first, groups, unroll):
    length, pairs_dev, heights = legendre.shape
    columns = coef.shape[2]
    slots = row_of_slot.shape[0]
    pairs = groups * GROUP
    return pl.pallas_call(
        functools.partial(
            legendre_kernel, length=length, first=first, pairs_dev=pairs_dev, unroll=unroll
        ),
        out_shape=jax.ShapeDtypeStruct((slots, 4, pairs, columns), jnp.bfloat16),
        grid_spec=pltpu.PrefetchScalarGridSpec(
            num_scalar_prefetch=1,
            grid=(groups,),
            in_specs=[
                pl.BlockSpec((slots,), lambda group, wave: (0,)),
                pl.BlockSpec((length, GROUP, heights), lambda group, wave: (0, first + group, 0)),
                pl.BlockSpec((length, GROUP, columns), lambda group, wave: (0, first + group, 0)),
            ],
            out_specs=pl.BlockSpec((slots, 4, GROUP, columns), lambda group, wave: (0, 0, group, 0)),
            scratch_shapes=[
                pltpu.VMEM((slots, heights), jnp.bfloat16),
                pltpu.VMEM((pl.cdiv(heights, LANES), length * GROUP, LANES), jnp.float32),
                pltpu.VMEM((length * GROUP, columns), jnp.float32),
                pltpu.VMEM((4, slots * GROUP, columns), jnp.float32),
            ],
        ),
        compiler_params=pltpu.CompilerParams(vmem_limit_bytes=56 << 20),
        cost_estimate=pl.CostEstimate(
            flops=2 * pairs * 4 * columns * heights * (length + slots),
            bytes_accessed=2 * pairs * (length * (heights + columns) + slots * 4 * columns),
            transcendentals=0,
        ),
    )(m_of_pair, row_of_slot, legendre, coef)


def legendre_rows_plain(low_m, row_of_slot, legendre, coef):
    length = legendre.shape[0]
    fields = coef.shape[2] // 2
    position = jnp.arange(length, dtype=jnp.int32)[:, None]
    cut = (length - 1 - low_m)[None, :]
    in_low = position < cut
    parity = jnp.where(in_low, position, position + cut) % 2
    sign = jnp.where(parity == 0, 1.0, -1.0).astype(jnp.bfloat16)[:, :, None]
    kinds = []
    for keep in (in_low, ~in_low):
        kept = jnp.where(keep[:, :, None], coef, jnp.zeros((), coef.dtype))
        for part in range(2):
            values = kept[:, :, part * fields : (part + 1) * fields]
            kinds.append(jnp.concatenate([values, values * sign], axis=2))
    fourier = jnp.einsum(
        "kph,kpqc->hqpc", legendre, jnp.stack(kinds, axis=2), preferred_element_type=jnp.float32
    ).astype(jnp.bfloat16)
    taken = jnp.take(fourier, jnp.maximum(row_of_slot, 0), axis=0)
    return jnp.where((row_of_slot >= 0)[:, None, None, None], taken, jnp.zeros((), taken.dtype))


def dft_kernel(*refs, total):
    rows_ref, table_ref, *added, out_ref = refs
    for slot in range(out_ref.shape[0]):
        rows = rows_ref[:, slot].reshape(table_ref.shape[0], rows_ref.shape[3])
        values = lax.dot_general(
            rows, table_ref[...], (((0,), (0,)), ((), ())), preferred_element_type=jnp.float32
        ).reshape(out_ref.shape[1:])
        if total:
            values = values + added[0][slot]
        out_ref[slot] = values.astype(out_ref.dtype)


def dft_rows(rows, table, begin, *added, step=4):
    sources, slots, depth, columns = rows.shape
    depth = depth * sources
    total = bool(added)
    out_block = (step, 2, columns // 2, table.shape[1])
    out_spec = pl.BlockSpec(out_block, lambda block: (block, 0, 0, 0))
    return pl.pallas_call(
        functools.partial(dft_kernel, total=total),
        out_shape=jax.ShapeDtypeStruct(
            (slots,) + out_block[1:], jnp.bfloat16 if total else jnp.float32
        ),
        grid=(pl.cdiv(slots, step),),
        in_specs=[
            pl.BlockSpec((sources, step) + rows.shape[2:], lambda block: (0, block, 0, 0)),
            pl.BlockSpec(
                (depth, table.shape[1]),
                lambda block: (begin // depth, 0),
                pipeline_mode=pl.Buffered(1),
            ),
        ]
        + [out_spec] * len(added),
        out_specs=out_spec,
        compiler_params=pltpu.CompilerParams(vmem_limit_bytes=58 << 20),
        cost_estimate=pl.CostEstimate(
            flops=2 * slots * columns * depth * table.shape[1],
            bytes_accessed=2 * rows.size + (2 * depth + 6 * slots * columns) * table.shape[1],
            transcendentals=0,
        ),
    )(rows, table, *added)


def dft_rows_plain(rows, table):
    sources, slots, depth, columns = rows.shape
    values = jnp.einsum(
        "dlkc,dkj->lcj", rows, table.reshape(sources, depth, -1), preferred_element_type=jnp.float32
    )
    return values.astype(jnp.bfloat16).reshape(slots, 2, columns // 2, -1)


def dft_table(m_of_pair, wave_count, pairs_dev, cuts):
    low = m_of_pair.reshape(-1, 1, 1, pairs_dev)
    wave = jnp.concatenate([low, wave_count - 1 - low], axis=1)
    wave = jnp.broadcast_to(wave, (wave.shape[0], 2, 2, pairs_dev))
    shift = jnp.broadcast_to(jnp.array([0, NLON // 4], jnp.int32)[:, None], wave.shape)
    order = lambda values: jnp.concatenate(
        [values[..., begin:end].reshape(-1) for begin, end in cuts]
    )[:, None]
    wave, shift = order(wave), order(shift)
    longitude = jnp.arange(NLON, dtype=jnp.int32)
    angles = ((wave * longitude + shift) % NLON).astype(jnp.float32) * (2.0 * math.pi / NLON)
    weights = jnp.where(wave == 0, 1.0, 2.0).astype(jnp.float32)
    return (weights * jnp.cos(angles)).astype(jnp.bfloat16)


def dft_table_plain(m_of_pair, wave_count, pairs_dev):
    low = m_of_pair.reshape(-1, 1, pairs_dev)
    wave = jnp.concatenate([low, wave_count - 1 - low], axis=1)[..., None]
    longitude = jnp.arange(NLON, dtype=jnp.int32)
    angles = (wave * longitude % NLON).astype(jnp.float32) * (2.0 * math.pi / NLON)
    weights = jnp.where(wave == 0, 1.0, 2.0).astype(jnp.float32)
    table = jnp.stack([weights * jnp.cos(angles), -weights * jnp.sin(angles)], axis=2)
    return table.astype(jnp.bfloat16).reshape(-1, NLON)


def spectrum_terms(coef, low_m):
    pairs_dev, length, columns = coef.shape
    wave_count = length - 1
    fields = columns // 2
    squares = coef.astype(jnp.float32) ** 2
    power_sum = squares[:, :, :fields] + squares[:, :, fields:]
    padded = jnp.concatenate(
        [jnp.zeros((pairs_dev, wave_count, fields), jnp.float32), power_sum[:, :wave_count]], axis=1
    )
    shifted = jax.vmap(
        lambda values, offset: lax.dynamic_slice_in_dim(values, offset, wave_count, 0)
    )(padded, wave_count - low_m)
    degree = jnp.arange(wave_count, dtype=jnp.int32)
    high_keep = (degree[None, :] >= (wave_count - 1 - low_m)[:, None]).astype(jnp.float32)
    high_terms = power_sum[:, 1:] * high_keep[:, :, None]
    low_weight = jnp.where(low_m == 0, 1.0, 2.0).astype(jnp.float32)
    return jnp.sum(low_weight[:, None, None] * shifted + 2.0 * high_terms, axis=0)


def spectrum_kernel(wave_ref, coef_ref, after_ref, out_ref, coef32_ref, low_ref, high_ref, *, pairs_dev):
    group = pl.program_id(0)
    base = lax.axis_index("lat") * pairs_dev + group * GROUP
    length, _, columns = coef_ref.shape
    wave_count = length - 1

    @pl.when(group == 0)
    def _():
        low_ref[...] = jnp.zeros_like(low_ref)
        high_ref[...] = jnp.zeros_like(high_ref)

    coef32_ref[...] = coef_ref[...].astype(jnp.float32).reshape(coef32_ref.shape)
    position = lax.broadcasted_iota(jnp.int32, (length, columns), 0)

    @pl.loop(0, GROUP)
    def _(member):
        low = wave_ref[base + member]
        values = coef32_ref[pl.ds(member, length, stride=GROUP), :]
        power = values * values
        in_low = position < wave_count - low
        weight = jnp.where(low == 0, 1.0, 2.0)
        low_ref[pl.ds(low, length), :] += jnp.where(in_low, weight * power, 0.0)
        high_ref[...] += jnp.where(in_low, 0.0, 2.0 * power)

    @pl.when(group == pl.num_programs(0) - 1)
    def _():
        terms = low_ref[pl.ds(0, wave_count), :] + high_ref[pl.ds(1, wave_count), :]
        terms = terms + pltpu.roll(terms, columns // 2, 1)
        out_ref[...] = terms[:, : columns // 2]


def spectrum_sums(m_of_pair, coef, after):
    length, pairs_dev, columns = coef.shape
    spare = length + (m_of_pair.shape[0] + 7) // 8 * 8
    return pl.pallas_call(
        functools.partial(spectrum_kernel, pairs_dev=pairs_dev),
        out_shape=jax.ShapeDtypeStruct((length - 1, columns // 2), jnp.float32),
        grid_spec=pltpu.PrefetchScalarGridSpec(
            num_scalar_prefetch=1,
            grid=(pairs_dev // GROUP,),
            in_specs=[
                pl.BlockSpec((length, GROUP, columns), lambda group, wave: (0, group, 0)),
                pl.BlockSpec(memory_space=pl.ANY),
            ],
            out_specs=pl.BlockSpec((length - 1, columns // 2), lambda group, wave: (0, 0)),
            scratch_shapes=[
                pltpu.VMEM((length * GROUP, columns), jnp.float32),
                pltpu.VMEM((spare, columns), jnp.float32),
                pltpu.VMEM((length, columns), jnp.float32),
            ],
        ),
        compiler_params=pltpu.CompilerParams(vmem_limit_bytes=58 << 20),
        cost_estimate=pl.CostEstimate(
            flops=8 * coef.size, bytes_accessed=2 * coef.size, transcendentals=0
        ),
    )(m_of_pair, coef, after)


def sum_kernel(own_ref, *refs, scale):
    *got, _, out_ref = refs
    summed = own_ref[...]
    for piece in got:
        summed = summed + piece[...]
    if scale:
        first = lax.axis_index("lat") * own_ref.shape[0]
        degree = (first + lax.broadcasted_iota(jnp.int32, own_ref.shape, 0)).astype(jnp.float32)
        summed = summed * (scale / (2.0 * degree + 1.0))
    out_ref[...] = summed


def sum_pieces(pieces, after, scale=0):
    shape = pieces[0].shape
    whole = pl.BlockSpec(shape, lambda: (0, 0))
    return pl.pallas_call(
        functools.partial(sum_kernel, scale=scale),
        out_shape=jax.ShapeDtypeStruct(shape, pieces[0].dtype),
        in_specs=[whole] * len(pieces) + [pl.BlockSpec(memory_space=pl.ANY)],
        out_specs=whole,
        compiler_params=pltpu.CompilerParams(vmem_limit_bytes=58 << 20),
    )(*pieces, after)


def scatter_round(terms, sources, stride, members):
    index = lax.axis_index("lat") // stride % members
    axis = 1 if stride == 1 and terms.ndim == 4 else 0
    mine = lambda step: lax.dynamic_index_in_dim(terms, index ^ step, axis, keepdims=False)
    pieces = [mine(0)]
    for step in range(1, members):
        pairs = [(i, i ^ (step * stride)) for i in range(sources)]
        pieces.append(lax.ppermute(mine(step), "lat", pairs))
    return [piece.reshape(-1, terms.shape[-1]) for piece in pieces]


def exchange(outgoing, sources):
    incoming = lax.all_to_all(
        outgoing.reshape(outgoing.shape[0], -1, outgoing.shape[3]), "lat", split_axis=0, concat_axis=0, tiled=True
    )
    return incoming.reshape((sources, -1) + incoming.shape[1:])


def local(coef, legendre, m_of_pair, row_of_slot):
    pairs_dev, length, columns = coef.shape
    wave_count = length - 1
    device = lax.axis_index("lat")
    sources = m_of_pair.shape[0] // pairs_dev
    low_m = lax.dynamic_slice_in_dim(m_of_pair, device * pairs_dev, pairs_dev)
    legend_rows = jnp.transpose(legendre, (1, 0, 2))
    coef_rows = jnp.transpose(coef, (1, 0, 2))
    if pairs_dev % GROUP == 0 and pairs_dev > GROUP and sources == 16:
        groups = pairs_dev // GROUP
        rest = pairs_dev - GROUP
        head = functools.partial(legendre_rows, m_of_pair, row_of_slot, legend_rows, coef_rows)
        outgoing = head(groups - 1, 1, 4)
        first_in = exchange(outgoing, sources)
        second_in = exchange(head(0, groups - 1, 2), sources)
        table = dft_table(m_of_pair, wave_count, pairs_dev, ((0, rest), (rest, pairs_dev)))
        partial = dft_rows(first_in, table, 4 * sources * rest)
        grid_out = dft_rows(second_in, table, 0, partial)
        terms = spectrum_sums(m_of_pair, coef_rows, outgoing)
        terms = terms.reshape(sources // 4, 4, -1, columns // 2)
        terms = sum_pieces(scatter_round(terms, sources, 1, 4), partial)
        terms = terms.reshape(sources // 4, -1, columns // 2)
        pieces = scatter_round(terms, sources, 4, sources // 4)
        spectrum = sum_pieces(pieces, grid_out, wave_count)
    else:
        outgoing = legendre_rows_plain(low_m, row_of_slot, legend_rows, coef_rows)
        table = dft_table_plain(m_of_pair, wave_count, pairs_dev)
        grid_out = dft_rows_plain(exchange(outgoing, sources), table)
        terms = spectrum_terms(coef, low_m)
        summed = lax.psum_scatter(terms, "lat", scatter_dimension=0, tiled=True)
        local_degree = (
            device * summed.shape[0] + jnp.arange(summed.shape[0], dtype=jnp.int32)
        ).astype(jnp.float32)
        spectrum = summed * (wave_count / (2.0 * local_degree + 1.0))[:, None]
    return (grid_out, spectrum)


def solution(mesh):
    in_specs = (P("lat", None, "slab"), P("lat", None, None), P(), P())
    out_specs = (P("lat", None, "slab", None), P("lat", "slab"))
    return jax.shard_map(local, mesh=mesh, in_specs=in_specs, out_specs=out_specs, check_vma=False)
```

```python
import functools
import math

import jax
import jax.numpy as jnp
from jax import lax
from jax.experimental import pallas as pl
from jax.experimental.pallas import tpu as pltpu
from jax.sharding import PartitionSpec as P

NLON = 1440
GROUP = 8
STEP = 4
LANES = 128


def legendre_kernel(
    wave_ref, slot_ref, leg_ref, coef_ref, *refs, length, first, pairs_dev, unroll
):
    *out_refs, pick_ref, leg32_ref, coef32_ref, rows_ref = refs
    group = pl.program_id(0)
    base = lax.axis_index("lat") * pairs_dev + (first + group) * GROUP
    slots, heights = pick_ref.shape
    columns = coef_ref.shape[2]
    fields = columns // 2
    tiles = leg32_ref.shape[0]

    @pl.when(group == 0)
    def _():
        height = lax.broadcasted_iota(jnp.int32, (heights, slots), 0)
        pick_ref[...] = jnp.transpose(jnp.where(height == slot_ref[...].reshape(1, slots), 1.0, 0.0)).astype(jnp.bfloat16)

    for tile in range(tiles):
        start = tile * LANES
        width = min(LANES, heights - start)
        piece = leg_ref[:, :, start : start + width].astype(jnp.float32)
        leg32_ref[tile, :, :width] = piece.reshape(length * GROUP, width)
    coef32_ref[...] = coef_ref[...].astype(jnp.float32).reshape(coef32_ref.shape)
    even = length - 1
    position = lax.broadcasted_iota(jnp.int32, (1, even), 1)

    def one_pair(member):
        low = wave_ref[base + member]
        cut = even - low
        pick_rows = pl.ds(member, even, stride=GROUP)
        leg = jnp.concatenate([leg32_ref[tile, pick_rows, :] for tile in range(tiles)], axis=1)
        leg = leg[:, :heights].astype(jnp.bfloat16)
        coef = jnp.transpose(coef32_ref[pick_rows, :]).astype(jnp.bfloat16)
        in_low = position < cut
        operand = []
        for segment in range(2):
            keep = in_low if segment == 0 else jnp.logical_not(in_low)
            parity = lax.rem(position if segment == 0 else position + cut, 2)
            north = jnp.where(keep, 1.0, 0.0)
            south = jnp.where(parity == 0, north, -north).astype(jnp.bfloat16)
            north = north.astype(jnp.bfloat16)
            for part in range(2):
                values = coef[part * fields : (part + 1) * fields]
                operand += [values * north, values * south]
        operand = jnp.concatenate(operand, axis=0)
        fourier = jnp.dot(operand, leg, preferred_element_type=jnp.float32)
        last_row = pl.ds(even * GROUP + member, 1)
        last_leg = jnp.concatenate([leg32_ref[tile, last_row, :] for tile in range(tiles)], axis=1)
        last_coef = jnp.transpose(coef32_ref[last_row, :])
        sign = jnp.where(lax.rem(low, 2) == 0, 1.0, -1.0)
        halves = [last_coef[:fields], last_coef[fields:]]
        last = jnp.concatenate([v for h in halves for v in (h, h * sign)], axis=0)
        high = fourier[2 * columns :] + last * last_leg[:, :heights]
        fourier = jnp.concatenate([fourier[: 2 * columns], high], axis=0).astype(jnp.bfloat16)
        taken = lax.dot_general(
            pick_ref[...], fourier, (((1,), (1,)), ((), ())), preferred_element_type=jnp.float32
        )
        for kind in range(4):
            rows_ref[kind, pl.ds(member, slots, stride=GROUP), :] = taken[
                :, kind * columns : (kind + 1) * columns
            ]

    @pl.loop(0, GROUP // unroll)
    def _(step):
        for turn in range(unroll):
            one_pair(step * unroll + turn)

    begin = 0
    for out_ref in out_refs:
        count = out_ref.shape[0]
        for kind in range(4):
            values = rows_ref[kind, begin * GROUP : (begin + count) * GROUP, :]
            out_ref[:, kind] = values.reshape(count, GROUP, columns).astype(jnp.bfloat16)
        begin += count


def legendre_rows(m_of_pair, legendre, coef, row_of_slot, parts, first, groups, unroll):
    length, pairs_dev, heights = legendre.shape
    columns = coef.shape[2]
    slots = row_of_slot.shape[0]
    pairs = groups * GROUP
    return pl.pallas_call(
        functools.partial(
            legendre_kernel, length=length, first=first, pairs_dev=pairs_dev, unroll=unroll
        ),
        out_shape=[jax.ShapeDtypeStruct((part, 4, pairs, columns), jnp.bfloat16) for part in parts],
        grid_spec=pltpu.PrefetchScalarGridSpec(
            num_scalar_prefetch=1,
            grid=(groups,),
            in_specs=[
                pl.BlockSpec((slots,), lambda group, wave: (0,)),
                pl.BlockSpec((length, GROUP, heights), lambda group, wave: (0, first + group, 0)),
                pl.BlockSpec((length, GROUP, columns), lambda group, wave: (0, first + group, 0)),
            ],
            out_specs=[
                pl.BlockSpec((part, 4, GROUP, columns), lambda group, wave: (0, 0, group, 0))
                for part in parts
            ],
            scratch_shapes=[
                pltpu.VMEM((slots, heights), jnp.bfloat16),
                pltpu.VMEM((pl.cdiv(heights, LANES), length * GROUP, LANES), jnp.float32),
                pltpu.VMEM((length * GROUP, columns), jnp.float32),
                pltpu.VMEM((4, slots * GROUP, columns), jnp.float32),
            ],
        ),
        compiler_params=pltpu.CompilerParams(vmem_limit_bytes=56 << 20),
        cost_estimate=pl.CostEstimate(
            flops=2 * pairs * 4 * columns * heights * (length + slots),
            bytes_accessed=2 * pairs * (length * (heights + columns) + slots * 4 * columns),
            transcendentals=0,
        ),
    )(m_of_pair, row_of_slot, legendre, coef)


def legendre_rows_plain(low_m, row_of_slot, legendre, coef):
    length = legendre.shape[0]
    fields = coef.shape[2] // 2
    position = jnp.arange(length, dtype=jnp.int32)[:, None]
    cut = (length - 1 - low_m)[None, :]
    in_low = position < cut
    parity = jnp.where(in_low, position, position + cut) % 2
    sign = jnp.where(parity == 0, 1.0, -1.0).astype(jnp.bfloat16)[:, :, None]
    kinds = []
    for keep in (in_low, ~in_low):
        kept = jnp.where(keep[:, :, None], coef, jnp.zeros((), coef.dtype))
        for part in range(2):
            values = kept[:, :, part * fields : (part + 1) * fields]
            kinds.append(jnp.concatenate([values, values * sign], axis=2))
    fourier = jnp.einsum(
        "kph,kpqc->hqpc", legendre, jnp.stack(kinds, axis=2), preferred_element_type=jnp.float32
    ).astype(jnp.bfloat16)
    taken = jnp.take(fourier, jnp.maximum(row_of_slot, 0), axis=0)
    return jnp.where((row_of_slot >= 0)[:, None, None, None], taken, jnp.zeros((), taken.dtype))


def dft_kernel(rows_ref, table_ref, *refs):
    *others, out_ref = refs
    for slot in range(out_ref.shape[0]):
        rows = rows_ref[:, slot].reshape(table_ref.shape[0], rows_ref.shape[3])
        values = lax.dot_general(
            rows, table_ref[...], (((0,), (0,)), ((), ())), preferred_element_type=jnp.float32
        ).reshape(out_ref.shape[1:])
        if others:
            values = values + others[0][slot]
        out_ref[slot] = values.astype(out_ref.dtype)


def dft_rows(rows, table, begin, total, first, step, *others):
    sources, slots, depth, columns = rows.shape
    depth = depth * sources
    out_block = (step, 2, columns // 2, table.shape[1])
    out_spec = pl.BlockSpec(out_block, lambda block: (first // step + block, 0, 0, 0))
    return pl.pallas_call(
        dft_kernel,
        out_shape=jax.ShapeDtypeStruct(
            (total,) + out_block[1:], jnp.bfloat16 if others else jnp.float32
        ),
        grid=(pl.cdiv(slots, step),),
        in_specs=[
            pl.BlockSpec((sources, step) + rows.shape[2:], lambda block: (0, block, 0, 0)),
            pl.BlockSpec(
                (depth, table.shape[1]),
                lambda block: (begin // depth, 0),
                pipeline_mode=pl.Buffered(1),
            ),
        ]
        + [out_spec, pl.BlockSpec(memory_space=pl.ANY)][: len(others)],
        out_specs=out_spec,
        input_output_aliases={3: 0} if len(others) > 1 else {},
        compiler_params=pltpu.CompilerParams(vmem_limit_bytes=58 << 20),
        cost_estimate=pl.CostEstimate(
            flops=2 * slots * columns * depth * table.shape[1],
            bytes_accessed=2 * rows.size + (2 * depth + 6 * slots * columns) * table.shape[1],
            transcendentals=0,
        ),
    )(rows, table, *others)


def dft_rows_plain(rows, table):
    sources, slots, depth, columns = rows.shape
    values = jnp.einsum(
        "dlkc,dkj->lcj", rows, table.reshape(sources, depth, -1), preferred_element_type=jnp.float32
    )
    return values.astype(jnp.bfloat16).reshape(slots, 2, columns // 2, -1)


def dft_table(m_of_pair, wave_count, pairs_dev, cuts):
    low = m_of_pair.reshape(-1, 1, 1, pairs_dev)
    wave = jnp.concatenate([low, wave_count - 1 - low], axis=1)
    wave = jnp.broadcast_to(wave, (wave.shape[0], 2, 2, pairs_dev))
    shift = jnp.broadcast_to(jnp.array([0, NLON // 4], jnp.int32)[:, None], wave.shape)
    order = lambda values: jnp.concatenate(
        [values[..., begin:end].reshape(-1) for begin, end in cuts]
    )[:, None]
    wave, shift = order(wave), order(shift)
    longitude = jnp.arange(NLON, dtype=jnp.int32)
    angles = ((wave * longitude + shift) % NLON).astype(jnp.float32) * (2.0 * math.pi / NLON)
    weights = jnp.where(wave == 0, 1.0, 2.0).astype(jnp.float32)
    return (weights * jnp.cos(angles)).astype(jnp.bfloat16)


def dft_table_plain(m_of_pair, wave_count, pairs_dev):
    low = m_of_pair.reshape(-1, 1, pairs_dev)
    wave = jnp.concatenate([low, wave_count - 1 - low], axis=1)[..., None]
    longitude = jnp.arange(NLON, dtype=jnp.int32)
    angles = (wave * longitude % NLON).astype(jnp.float32) * (2.0 * math.pi / NLON)
    weights = jnp.where(wave == 0, 1.0, 2.0).astype(jnp.float32)
    table = jnp.stack([weights * jnp.cos(angles), -weights * jnp.sin(angles)], axis=2)
    return table.astype(jnp.bfloat16).reshape(-1, NLON)


def spectrum_terms(coef, low_m):
    pairs_dev, length, columns = coef.shape
    wave_count = length - 1
    fields = columns // 2
    squares = coef.astype(jnp.float32) ** 2
    power_sum = squares[:, :, :fields] + squares[:, :, fields:]
    padded = jnp.concatenate(
        [jnp.zeros((pairs_dev, wave_count, fields), jnp.float32), power_sum[:, :wave_count]], axis=1
    )
    shifted = jax.vmap(
        lambda values, offset: lax.dynamic_slice_in_dim(values, offset, wave_count, 0)
    )(padded, wave_count - low_m)
    degree = jnp.arange(wave_count, dtype=jnp.int32)
    high_keep = (degree[None, :] >= (wave_count - 1 - low_m)[:, None]).astype(jnp.float32)
    high_terms = power_sum[:, 1:] * high_keep[:, :, None]
    low_weight = jnp.where(low_m == 0, 1.0, 2.0).astype(jnp.float32)
    return jnp.sum(low_weight[:, None, None] * shifted + 2.0 * high_terms, axis=0)


def spectrum_kernel(wave_ref, coef_ref, after_ref, out_ref, coef32_ref, low_ref, high_ref, *, pairs_dev):
    group = pl.program_id(0)
    base = lax.axis_index("lat") * pairs_dev + group * GROUP
    length, _, columns = coef_ref.shape
    wave_count = length - 1

    @pl.when(group == 0)
    def _():
        low_ref[...] = jnp.zeros_like(low_ref)
        high_ref[...] = jnp.zeros_like(high_ref)

    coef32_ref[...] = coef_ref[...].astype(jnp.float32).reshape(coef32_ref.shape)
    position = lax.broadcasted_iota(jnp.int32, (length, columns), 0)

    @pl.loop(0, GROUP)
    def _(member):
        low = wave_ref[base + member]
        values = coef32_ref[pl.ds(member, length, stride=GROUP), :]
        power = values * values
        in_low = position < wave_count - low
        weight = jnp.where(low == 0, 1.0, 2.0)
        low_ref[pl.ds(low, length), :] += jnp.where(in_low, weight * power, 0.0)
        high_ref[...] += jnp.where(in_low, 0.0, 2.0 * power)

    @pl.when(group == pl.num_programs(0) - 1)
    def _():
        terms = low_ref[pl.ds(0, wave_count), :] + high_ref[pl.ds(1, wave_count), :]
        terms = terms + pltpu.roll(terms, columns // 2, 1)
        out_ref[...] = terms[:, : columns // 2]


def spectrum_sums(m_of_pair, coef, after):
    length, pairs_dev, columns = coef.shape
    spare = length + (m_of_pair.shape[0] + 7) // 8 * 8
    return pl.pallas_call(
        functools.partial(spectrum_kernel, pairs_dev=pairs_dev),
        out_shape=jax.ShapeDtypeStruct((length - 1, columns // 2), jnp.float32),
        grid_spec=pltpu.PrefetchScalarGridSpec(
            num_scalar_prefetch=1,
            grid=(pairs_dev // GROUP,),
            in_specs=[
                pl.BlockSpec((length, GROUP, columns), lambda group, wave: (0, group, 0)),
                pl.BlockSpec(memory_space=pl.ANY),
            ],
            out_specs=pl.BlockSpec((length - 1, columns // 2), lambda group, wave: (0, 0)),
            scratch_shapes=[
                pltpu.VMEM((length * GROUP, columns), jnp.float32),
                pltpu.VMEM((spare, columns), jnp.float32),
                pltpu.VMEM((length, columns), jnp.float32),
            ],
        ),
        compiler_params=pltpu.CompilerParams(vmem_limit_bytes=58 << 20),
        cost_estimate=pl.CostEstimate(
            flops=8 * coef.size, bytes_accessed=2 * coef.size, transcendentals=0
        ),
    )(m_of_pair, coef, after)


def sum_kernel(own_ref, *refs, scale):
    *got, _, out_ref = refs
    summed = own_ref[...]
    for piece in got:
        summed = summed + piece[...]
    if scale:
        first = lax.axis_index("lat") * own_ref.shape[0]
        degree = (first + lax.broadcasted_iota(jnp.int32, own_ref.shape, 0)).astype(jnp.float32)
        summed = summed * (scale / (2.0 * degree + 1.0))
    out_ref[...] = summed


def sum_pieces(pieces, after, scale=0):
    shape = pieces[0].shape
    whole = pl.BlockSpec(shape, lambda: (0, 0))
    return pl.pallas_call(
        functools.partial(sum_kernel, scale=scale),
        out_shape=jax.ShapeDtypeStruct(shape, pieces[0].dtype),
        in_specs=[whole] * len(pieces) + [pl.BlockSpec(memory_space=pl.ANY)],
        out_specs=whole,
        compiler_params=pltpu.CompilerParams(vmem_limit_bytes=58 << 20),
    )(*pieces, after)


def gate_kernel(*refs):
    pass


def gate(value, after):
    anywhere = pl.BlockSpec(memory_space=pl.ANY)
    return pl.pallas_call(
        gate_kernel,
        out_shape=jax.ShapeDtypeStruct(value.shape, value.dtype),
        in_specs=[anywhere, anywhere],
        out_specs=anywhere,
        input_output_aliases={0: 0},
        compiler_params=pltpu.CompilerParams(vmem_limit_bytes=58 << 20),
    )(value, after)


def scatter_round(terms, sources, stride, members):
    index = lax.axis_index("lat") // stride % members
    axis = 1 if stride == 1 and terms.ndim == 4 else 0
    mine = lambda step: lax.dynamic_index_in_dim(terms, index ^ step, axis, keepdims=False)
    pieces = [mine(0)]
    for step in range(1, members):
        pairs = [(i, i ^ (step * stride)) for i in range(sources)]
        pieces.append(lax.ppermute(mine(step), "lat", pairs))
    return [piece.reshape(-1, terms.shape[-1]) for piece in pieces]


def exchange(outgoing, sources):
    incoming = lax.all_to_all(
        outgoing.reshape(outgoing.shape[0], -1, outgoing.shape[3]), "lat", split_axis=0, concat_axis=0, tiled=True
    )
    return incoming.reshape((sources, -1) + incoming.shape[1:])


def local(coef, legendre, m_of_pair, row_of_slot):
    pairs_dev, length, columns = coef.shape
    wave_count = length - 1
    device = lax.axis_index("lat")
    sources = m_of_pair.shape[0] // pairs_dev
    low_m = lax.dynamic_slice_in_dim(m_of_pair, device * pairs_dev, pairs_dev)
    legend_rows = jnp.transpose(legendre, (1, 0, 2))
    coef_rows = jnp.transpose(coef, (1, 0, 2))
    if pairs_dev % GROUP == 0 and pairs_dev > GROUP and sources == 16 and row_of_slot.shape[0] % (sources * STEP):
        groups = pairs_dev // GROUP
        rest = pairs_dev - GROUP
        head = functools.partial(legendre_rows, m_of_pair, legend_rows, coef_rows)
        slots = row_of_slot.shape[0]
        slots_dev = slots // sources
        main = slots_dev - slots_dev % STEP
        (outgoing,) = head(row_of_slot, [slots], groups - 1, 1, 4)
        first_in = exchange(outgoing, sources)
        by_device = row_of_slot.reshape(sources, slots_dev)
        order = jnp.concatenate([by_device[:, :main].reshape(-1), by_device[:, main:].reshape(-1)])
        main_out, last_out = head(
            order, [sources * main, sources * (slots_dev - main)], 0, groups - 1, 2
        )
        main_in = exchange(main_out, sources)
        table = dft_table(m_of_pair, wave_count, pairs_dev, ((0, rest), (rest, pairs_dev)))
        partial = dft_rows(first_in, table, 4 * sources * rest, slots_dev, 0, STEP)
        grid_out = dft_rows(main_in, table, 0, slots_dev, 0, STEP, partial)
        terms = spectrum_sums(m_of_pair, coef_rows, outgoing)
        terms = terms.reshape(sources // 4, 4, -1, columns // 2)
        terms = sum_pieces(scatter_round(terms, sources, 1, 4), partial)
        last_in = exchange(gate(last_out, terms), sources)
        grid_out = dft_rows(last_in, table, 0, slots_dev, main, 1, partial, grid_out)
        terms = terms.reshape(sources // 4, -1, columns // 2)
        pieces = scatter_round(terms, sources, 4, sources // 4)
        spectrum = sum_pieces(pieces, grid_out, wave_count)
    else:
        outgoing = legendre_rows_plain(low_m, row_of_slot, legend_rows, coef_rows)
        table = dft_table_plain(m_of_pair, wave_count, pairs_dev)
        grid_out = dft_rows_plain(exchange(outgoing, sources), table)
        terms = spectrum_terms(coef, low_m)
        summed = lax.psum_scatter(terms, "lat", scatter_dimension=0, tiled=True)
        local_degree = (
            device * summed.shape[0] + jnp.arange(summed.shape[0], dtype=jnp.int32)
        ).astype(jnp.float32)
        spectrum = summed * (wave_count / (2.0 * local_degree + 1.0))[:, None]
    return (grid_out, spectrum)


def solution(mesh):
    in_specs = (P("lat", None, "slab"), P("lat", None, None), P(), P())
    out_specs = (P("lat", None, "slab", None), P("lat", "slab"))
    return jax.shard_map(local, mesh=mesh, in_specs=in_specs, out_specs=out_specs, check_vma=False)
```

```python
import functools
import math

import jax
import jax.numpy as jnp
from jax import lax
from jax.experimental import pallas as pl
from jax.experimental.pallas import tpu as pltpu
from jax.sharding import PartitionSpec as P

NLON = 1440
GROUP = 8
STEP = 3
LANES = 128


def legendre_kernel(
    wave_ref, slot_ref, leg_ref, coef_ref, *refs, length, first, pairs_dev, unroll
):
    *out_refs, pick_ref, leg32_ref, coef32_ref, rows_ref = refs
    group = pl.program_id(0)
    base = lax.axis_index("lat") * pairs_dev + (first + group) * GROUP
    slots, heights = pick_ref.shape
    columns = coef_ref.shape[2]
    fields = columns // 2
    tiles = leg32_ref.shape[0]

    @pl.when(group == 0)
    def _():
        height = lax.broadcasted_iota(jnp.int32, (heights, slots), 0)
        pick_ref[...] = jnp.transpose(jnp.where(height == slot_ref[...].reshape(1, slots), 1.0, 0.0)).astype(jnp.bfloat16)

    for tile in range(tiles):
        start = tile * LANES
        width = min(LANES, heights - start)
        piece = leg_ref[:, :, start : start + width].astype(jnp.float32)
        leg32_ref[tile, :, :width] = piece.reshape(length * GROUP, width)
    coef32_ref[...] = coef_ref[...].astype(jnp.float32).reshape(coef32_ref.shape)
    even = length - 1
    position = lax.broadcasted_iota(jnp.int32, (1, even), 1)

    def one_pair(member):
        low = wave_ref[base + member]
        cut = even - low
        pick_rows = pl.ds(member, even, stride=GROUP)
        leg = jnp.concatenate([leg32_ref[tile, pick_rows, :] for tile in range(tiles)], axis=1)
        leg = leg[:, :heights].astype(jnp.bfloat16)
        coef = jnp.transpose(coef32_ref[pick_rows, :]).astype(jnp.bfloat16)
        in_low = position < cut
        operand = []
        for segment in range(2):
            keep = in_low if segment == 0 else jnp.logical_not(in_low)
            parity = lax.rem(position if segment == 0 else position + cut, 2)
            north = jnp.where(keep, 1.0, 0.0)
            south = jnp.where(parity == 0, north, -north).astype(jnp.bfloat16)
            north = north.astype(jnp.bfloat16)
            for part in range(2):
                values = coef[part * fields : (part + 1) * fields]
                operand += [values * north, values * south]
        operand = jnp.concatenate(operand, axis=0)
        fourier = jnp.dot(operand, leg, preferred_element_type=jnp.float32)
        last_row = pl.ds(even * GROUP + member, 1)
        last_leg = jnp.concatenate([leg32_ref[tile, last_row, :] for tile in range(tiles)], axis=1)
        last_coef = jnp.transpose(coef32_ref[last_row, :])
        sign = jnp.where(lax.rem(low, 2) == 0, 1.0, -1.0)
        halves = [last_coef[:fields], last_coef[fields:]]
        last = jnp.concatenate([v for h in halves for v in (h, h * sign)], axis=0)
        high = fourier[2 * columns :] + last * last_leg[:, :heights]
        fourier = jnp.concatenate([fourier[: 2 * columns], high], axis=0).astype(jnp.bfloat16)
        taken = lax.dot_general(
            pick_ref[...], fourier, (((1,), (1,)), ((), ())), preferred_element_type=jnp.float32
        )
        for kind in range(4):
            rows_ref[kind, pl.ds(member, slots, stride=GROUP), :] = taken[
                :, kind * columns : (kind + 1) * columns
            ]

    @pl.loop(0, GROUP // unroll)
    def _(step):
        for turn in range(unroll):
            one_pair(step * unroll + turn)

    begin = 0
    for out_ref in out_refs:
        count = out_ref.shape[0]
        for kind in range(4):
            values = rows_ref[kind, begin * GROUP : (begin + count) * GROUP, :]
            out_ref[:, kind] = values.reshape(count, GROUP, columns).astype(jnp.bfloat16)
        begin += count


def legendre_rows(m_of_pair, legendre, coef, row_of_slot, parts, first, groups, unroll):
    length, pairs_dev, heights = legendre.shape
    columns = coef.shape[2]
    slots = row_of_slot.shape[0]
    pairs = groups * GROUP
    return pl.pallas_call(
        functools.partial(
            legendre_kernel, length=length, first=first, pairs_dev=pairs_dev, unroll=unroll
        ),
        out_shape=[jax.ShapeDtypeStruct((part, 4, pairs, columns), jnp.bfloat16) for part in parts],
        grid_spec=pltpu.PrefetchScalarGridSpec(
            num_scalar_prefetch=1,
            grid=(groups,),
            in_specs=[
                pl.BlockSpec((slots,), lambda group, wave: (0,)),
                pl.BlockSpec((length, GROUP, heights), lambda group, wave: (0, first + group, 0)),
                pl.BlockSpec((length, GROUP, columns), lambda group, wave: (0, first + group, 0)),
            ],
            out_specs=[
                pl.BlockSpec((part, 4, GROUP, columns), lambda group, wave: (0, 0, group, 0))
                for part in parts
            ],
            scratch_shapes=[
                pltpu.VMEM((slots, heights), jnp.bfloat16),
                pltpu.VMEM((pl.cdiv(heights, LANES), length * GROUP, LANES), jnp.float32),
                pltpu.VMEM((length * GROUP, columns), jnp.float32),
                pltpu.VMEM((4, slots * GROUP, columns), jnp.float32),
            ],
        ),
        compiler_params=pltpu.CompilerParams(vmem_limit_bytes=56 << 20),
        cost_estimate=pl.CostEstimate(
            flops=2 * pairs * 4 * columns * heights * (length + slots),
            bytes_accessed=2 * pairs * (length * (heights + columns) + slots * 4 * columns),
            transcendentals=0,
        ),
    )(m_of_pair, row_of_slot, legendre, coef)


def legendre_rows_plain(low_m, row_of_slot, legendre, coef):
    length = legendre.shape[0]
    fields = coef.shape[2] // 2
    position = jnp.arange(length, dtype=jnp.int32)[:, None]
    cut = (length - 1 - low_m)[None, :]
    in_low = position < cut
    parity = jnp.where(in_low, position, position + cut) % 2
    sign = jnp.where(parity == 0, 1.0, -1.0).astype(jnp.bfloat16)[:, :, None]
    kinds = []
    for keep in (in_low, ~in_low):
        kept = jnp.where(keep[:, :, None], coef, jnp.zeros((), coef.dtype))
        for part in range(2):
            values = kept[:, :, part * fields : (part + 1) * fields]
            kinds.append(jnp.concatenate([values, values * sign], axis=2))
    fourier = jnp.einsum(
        "kph,kpqc->hqpc", legendre, jnp.stack(kinds, axis=2), preferred_element_type=jnp.float32
    ).astype(jnp.bfloat16)
    taken = jnp.take(fourier, jnp.maximum(row_of_slot, 0), axis=0)
    return jnp.where((row_of_slot >= 0)[:, None, None, None], taken, jnp.zeros((), taken.dtype))


def dft_kernel(rows_ref, table_ref, *refs):
    *others, out_ref = refs
    for slot in range(out_ref.shape[0]):
        rows = rows_ref[:, slot].reshape(table_ref.shape[0], rows_ref.shape[3])
        values = lax.dot_general(
            rows, table_ref[...], (((0,), (0,)), ((), ())), preferred_element_type=jnp.float32
        ).reshape(out_ref.shape[1:])
        if others:
            values = values + others[0][slot]
        out_ref[slot] = values.astype(out_ref.dtype)


def dft_rows(rows, table, begin, total, first, step, *others):
    sources, slots, depth, columns = rows.shape
    depth = depth * sources
    out_block = (step, 2, columns // 2, table.shape[1])
    out_spec = pl.BlockSpec(out_block, lambda block: (first // step + block, 0, 0, 0))
    return pl.pallas_call(
        dft_kernel,
        out_shape=jax.ShapeDtypeStruct(
            (total,) + out_block[1:], jnp.bfloat16 if others else jnp.float32
        ),
        grid=(pl.cdiv(slots, step),),
        in_specs=[
            pl.BlockSpec((sources, step) + rows.shape[2:], lambda block: (0, block, 0, 0)),
            pl.BlockSpec(
                (depth, table.shape[1]),
                lambda block: (begin // depth, 0),
                pipeline_mode=pl.Buffered(1),
            ),
        ]
        + [out_spec, pl.BlockSpec(memory_space=pl.ANY)][: len(others)],
        out_specs=out_spec,
        input_output_aliases={3: 0} if len(others) > 1 else {},
        compiler_params=pltpu.CompilerParams(vmem_limit_bytes=58 << 20),
        cost_estimate=pl.CostEstimate(
            flops=2 * slots * columns * depth * table.shape[1],
            bytes_accessed=2 * rows.size + (2 * depth + 6 * slots * columns) * table.shape[1],
            transcendentals=0,
        ),
    )(rows, table, *others)


def dft_rows_plain(rows, table):
    sources, slots, depth, columns = rows.shape
    values = jnp.einsum(
        "dlkc,dkj->lcj", rows, table.reshape(sources, depth, -1), preferred_element_type=jnp.float32
    )
    return values.astype(jnp.bfloat16).reshape(slots, 2, columns // 2, -1)


def dft_table(m_of_pair, wave_count, pairs_dev, cuts):
    low = m_of_pair.reshape(-1, 1, 1, pairs_dev)
    wave = jnp.concatenate([low, wave_count - 1 - low], axis=1)
    wave = jnp.broadcast_to(wave, (wave.shape[0], 2, 2, pairs_dev))
    shift = jnp.broadcast_to(jnp.array([0, NLON // 4], jnp.int32)[:, None], wave.shape)
    order = lambda values: jnp.concatenate(
        [values[..., begin:end].reshape(-1) for begin, end in cuts]
    )[:, None]
    wave, shift = order(wave), order(shift)
    longitude = jnp.arange(NLON, dtype=jnp.int32)
    angles = ((wave * longitude + shift) % NLON).astype(jnp.float32) * (2.0 * math.pi / NLON)
    weights = jnp.where(wave == 0, 1.0, 2.0).astype(jnp.float32)
    return (weights * jnp.cos(angles)).astype(jnp.bfloat16)


def dft_table_plain(m_of_pair, wave_count, pairs_dev):
    low = m_of_pair.reshape(-1, 1, pairs_dev)
    wave = jnp.concatenate([low, wave_count - 1 - low], axis=1)[..., None]
    longitude = jnp.arange(NLON, dtype=jnp.int32)
    angles = (wave * longitude % NLON).astype(jnp.float32) * (2.0 * math.pi / NLON)
    weights = jnp.where(wave == 0, 1.0, 2.0).astype(jnp.float32)
    table = jnp.stack([weights * jnp.cos(angles), -weights * jnp.sin(angles)], axis=2)
    return table.astype(jnp.bfloat16).reshape(-1, NLON)


def spectrum_terms(coef, low_m):
    pairs_dev, length, columns = coef.shape
    wave_count = length - 1
    fields = columns // 2
    squares = coef.astype(jnp.float32) ** 2
    power_sum = squares[:, :, :fields] + squares[:, :, fields:]
    padded = jnp.concatenate(
        [jnp.zeros((pairs_dev, wave_count, fields), jnp.float32), power_sum[:, :wave_count]], axis=1
    )
    shifted = jax.vmap(
        lambda values, offset: lax.dynamic_slice_in_dim(values, offset, wave_count, 0)
    )(padded, wave_count - low_m)
    degree = jnp.arange(wave_count, dtype=jnp.int32)
    high_keep = (degree[None, :] >= (wave_count - 1 - low_m)[:, None]).astype(jnp.float32)
    high_terms = power_sum[:, 1:] * high_keep[:, :, None]
    low_weight = jnp.where(low_m == 0, 1.0, 2.0).astype(jnp.float32)
    return jnp.sum(low_weight[:, None, None] * shifted + 2.0 * high_terms, axis=0)


def spectrum_kernel(wave_ref, coef_ref, after_ref, out_ref, coef32_ref, low_ref, high_ref, *, pairs_dev):
    group = pl.program_id(0)
    base = lax.axis_index("lat") * pairs_dev + group * GROUP
    length, _, columns = coef_ref.shape
    wave_count = length - 1

    @pl.when(group == 0)
    def _():
        low_ref[...] = jnp.zeros_like(low_ref)
        high_ref[...] = jnp.zeros_like(high_ref)

    coef32_ref[...] = coef_ref[...].astype(jnp.float32).reshape(coef32_ref.shape)
    position = lax.broadcasted_iota(jnp.int32, (length, columns), 0)

    @pl.loop(0, GROUP)
    def _(member):
        low = wave_ref[base + member]
        values = coef32_ref[pl.ds(member, length, stride=GROUP), :]
        power = values * values
        in_low = position < wave_count - low
        weight = jnp.where(low == 0, 1.0, 2.0)
        low_ref[pl.ds(low, length), :] += jnp.where(in_low, weight * power, 0.0)
        high_ref[...] += jnp.where(in_low, 0.0, 2.0 * power)

    @pl.when(group == pl.num_programs(0) - 1)
    def _():
        terms = low_ref[pl.ds(0, wave_count), :] + high_ref[pl.ds(1, wave_count), :]
        terms = terms + pltpu.roll(terms, columns // 2, 1)
        out_ref[...] = terms[:, : columns // 2]


def spectrum_sums(m_of_pair, coef, after):
    length, pairs_dev, columns = coef.shape
    spare = length + (m_of_pair.shape[0] + 7) // 8 * 8
    return pl.pallas_call(
        functools.partial(spectrum_kernel, pairs_dev=pairs_dev),
        out_shape=jax.ShapeDtypeStruct((length - 1, columns // 2), jnp.float32),
        grid_spec=pltpu.PrefetchScalarGridSpec(
            num_scalar_prefetch=1,
            grid=(pairs_dev // GROUP,),
            in_specs=[
                pl.BlockSpec((length, GROUP, columns), lambda group, wave: (0, group, 0)),
                pl.BlockSpec(memory_space=pl.ANY),
            ],
            out_specs=pl.BlockSpec((length - 1, columns // 2), lambda group, wave: (0, 0)),
            scratch_shapes=[
                pltpu.VMEM((length * GROUP, columns), jnp.float32),
                pltpu.VMEM((spare, columns), jnp.float32),
                pltpu.VMEM((length, columns), jnp.float32),
            ],
        ),
        compiler_params=pltpu.CompilerParams(vmem_limit_bytes=58 << 20),
        cost_estimate=pl.CostEstimate(
            flops=8 * coef.size, bytes_accessed=2 * coef.size, transcendentals=0
        ),
    )(m_of_pair, coef, after)


def sum_kernel(own_ref, *refs, scale):
    *got, _, out_ref = refs
    summed = own_ref[...]
    for piece in got:
        summed = summed + piece[...]
    if scale:
        first = lax.axis_index("lat") * own_ref.shape[0]
        degree = (first + lax.broadcasted_iota(jnp.int32, own_ref.shape, 0)).astype(jnp.float32)
        summed = summed * (scale / (2.0 * degree + 1.0))
    out_ref[...] = summed


def sum_pieces(pieces, after, scale=0):
    shape = pieces[0].shape
    whole = pl.BlockSpec(shape, lambda: (0, 0))
    return pl.pallas_call(
        functools.partial(sum_kernel, scale=scale),
        out_shape=jax.ShapeDtypeStruct(shape, pieces[0].dtype),
        in_specs=[whole] * len(pieces) + [pl.BlockSpec(memory_space=pl.ANY)],
        out_specs=whole,
        compiler_params=pltpu.CompilerParams(vmem_limit_bytes=58 << 20),
    )(*pieces, after)


def gate_kernel(*refs):
    pass


def gate(value, after):
    anywhere = pl.BlockSpec(memory_space=pl.ANY)
    return pl.pallas_call(
        gate_kernel,
        out_shape=jax.ShapeDtypeStruct(value.shape, value.dtype),
        in_specs=[anywhere, anywhere],
        out_specs=anywhere,
        input_output_aliases={0: 0},
        compiler_params=pltpu.CompilerParams(vmem_limit_bytes=58 << 20),
    )(value, after)


def scatter_round(terms, sources, stride, members):
    index = lax.axis_index("lat") // stride % members
    axis = 1 if stride == 1 and terms.ndim == 4 else 0
    mine = lambda step: lax.dynamic_index_in_dim(terms, index ^ step, axis, keepdims=False)
    pieces = [mine(0)]
    for step in range(1, members):
        pairs = [(i, i ^ (step * stride)) for i in range(sources)]
        pieces.append(lax.ppermute(mine(step), "lat", pairs))
    return [piece.reshape(-1, terms.shape[-1]) for piece in pieces]


def exchange(outgoing, sources):
    incoming = lax.all_to_all(
        outgoing.reshape(outgoing.shape[0], -1, outgoing.shape[3]), "lat", split_axis=0, concat_axis=0, tiled=True
    )
    return incoming.reshape((sources, -1) + incoming.shape[1:])


def local(coef, legendre, m_of_pair, row_of_slot):
    pairs_dev, length, columns = coef.shape
    wave_count = length - 1
    device = lax.axis_index("lat")
    sources = m_of_pair.shape[0] // pairs_dev
    low_m = lax.dynamic_slice_in_dim(m_of_pair, device * pairs_dev, pairs_dev)
    legend_rows = jnp.transpose(legendre, (1, 0, 2))
    coef_rows = jnp.transpose(coef, (1, 0, 2))
    if pairs_dev % GROUP == 0 and pairs_dev > GROUP and sources == 16 and row_of_slot.shape[0] % (sources * STEP):
        groups = pairs_dev // GROUP
        rest = pairs_dev - GROUP
        head = functools.partial(legendre_rows, m_of_pair, legend_rows, coef_rows)
        slots = row_of_slot.shape[0]
        slots_dev = slots // sources
        main = slots_dev - slots_dev % STEP
        (outgoing,) = head(row_of_slot, [slots], groups - 1, 1, 8)
        first_in = exchange(outgoing, sources)
        by_device = row_of_slot.reshape(sources, slots_dev)
        order = jnp.concatenate([by_device[:, :main].reshape(-1), by_device[:, main:].reshape(-1)])
        main_out, last_out = head(
            order, [sources * main, sources * (slots_dev - main)], 0, groups - 1, 2
        )
        main_in = exchange(main_out, sources)
        table = dft_table(m_of_pair, wave_count, pairs_dev, ((0, rest), (rest, pairs_dev)))
        partial = dft_rows(first_in, table, 4 * sources * rest, slots_dev, 0, STEP)
        grid_out = dft_rows(main_in, table, 0, slots_dev, 0, STEP, partial)
        terms = spectrum_sums(m_of_pair, coef_rows, outgoing)
        terms = terms.reshape(sources // 4, 4, -1, columns // 2)
        terms = sum_pieces(scatter_round(terms, sources, 1, 4), partial)
        terms = terms.reshape(sources // 4, -1, columns // 2)
        pieces = scatter_round(terms, sources, 4, sources // 4)
        last_in = exchange(gate(last_out, pieces[0]), sources)
        grid_out = dft_rows(last_in, table, 0, slots_dev, main, 1, partial, grid_out)
        spectrum = sum_pieces(pieces, grid_out, wave_count)
    else:
        outgoing = legendre_rows_plain(low_m, row_of_slot, legend_rows, coef_rows)
        table = dft_table_plain(m_of_pair, wave_count, pairs_dev)
        grid_out = dft_rows_plain(exchange(outgoing, sources), table)
        terms = spectrum_terms(coef, low_m)
        summed = lax.psum_scatter(terms, "lat", scatter_dimension=0, tiled=True)
        local_degree = (
            device * summed.shape[0] + jnp.arange(summed.shape[0], dtype=jnp.int32)
        ).astype(jnp.float32)
        spectrum = summed * (wave_count / (2.0 * local_degree + 1.0))[:, None]
    return (grid_out, spectrum)


def solution(mesh):
    in_specs = (P("lat", None, "slab"), P("lat", None, None), P(), P())
    out_specs = (P("lat", None, "slab", None), P("lat", "slab"))
    return jax.shard_map(local, mesh=mesh, in_specs=in_specs, out_specs=out_specs, check_vma=False)
```

```python
import functools
import math

import jax
import jax.numpy as jnp
from jax import lax
from jax.experimental import pallas as pl
from jax.experimental.pallas import tpu as pltpu
from jax.sharding import PartitionSpec as P

NLON = 1440
GROUP = 8
STEP = 4
LANES = 128


def legendre_kernel(
    wave_ref, slot_ref, leg_ref, coef_ref, *refs, length, first, pairs_dev, unroll
):
    *out_refs, pick_ref, leg32_ref, coef32_ref, rows_ref = refs
    group = pl.program_id(0)
    base = lax.axis_index("lat") * pairs_dev + (first + group) * GROUP
    slots, heights = pick_ref.shape
    columns = coef_ref.shape[2]
    fields = columns // 2
    tiles = leg32_ref.shape[0]

    @pl.when(group == 0)
    def _():
        height = lax.broadcasted_iota(jnp.int32, (heights, slots), 0)
        pick_ref[...] = jnp.transpose(jnp.where(height == slot_ref[...].reshape(1, slots), 1.0, 0.0)).astype(jnp.bfloat16)

    for tile in range(tiles):
        start = tile * LANES
        width = min(LANES, heights - start)
        piece = leg_ref[:, :, start : start + width].astype(jnp.float32)
        leg32_ref[tile, :, :width] = piece.reshape(length * GROUP, width)
    coef32_ref[...] = coef_ref[...].astype(jnp.float32).reshape(coef32_ref.shape)
    even = length - 1
    position = lax.broadcasted_iota(jnp.int32, (1, even), 1)

    def one_pair(member):
        low = wave_ref[base + member]
        cut = even - low
        pick_rows = pl.ds(member, even, stride=GROUP)
        leg = jnp.concatenate([leg32_ref[tile, pick_rows, :] for tile in range(tiles)], axis=1)
        leg = leg[:, :heights].astype(jnp.bfloat16)
        coef = jnp.transpose(coef32_ref[pick_rows, :]).astype(jnp.bfloat16)
        in_low = position < cut
        operand = []
        for segment in range(2):
            keep = in_low if segment == 0 else jnp.logical_not(in_low)
            parity = lax.rem(position if segment == 0 else position + cut, 2)
            north = jnp.where(keep, 1.0, 0.0)
            south = jnp.where(parity == 0, north, -north).astype(jnp.bfloat16)
            north = north.astype(jnp.bfloat16)
            for part in range(2):
                values = coef[part * fields : (part + 1) * fields]
                operand += [values * north, values * south]
        operand = jnp.concatenate(operand, axis=0)
        fourier = jnp.dot(operand, leg, preferred_element_type=jnp.float32)
        last_row = pl.ds(even * GROUP + member, 1)
        last_leg = jnp.concatenate([leg32_ref[tile, last_row, :] for tile in range(tiles)], axis=1)
        last_coef = jnp.transpose(coef32_ref[last_row, :])
        sign = jnp.where(lax.rem(low, 2) == 0, 1.0, -1.0)
        halves = [last_coef[:fields], last_coef[fields:]]
        last = jnp.concatenate([v for h in halves for v in (h, h * sign)], axis=0)
        high = fourier[2 * columns :] + last * last_leg[:, :heights]
        fourier = jnp.concatenate([fourier[: 2 * columns], high], axis=0).astype(jnp.bfloat16)
        taken = lax.dot_general(
            pick_ref[...], fourier, (((1,), (1,)), ((), ())), preferred_element_type=jnp.float32
        )
        for kind in range(4):
            rows_ref[kind, pl.ds(member, slots, stride=GROUP), :] = taken[
                :, kind * columns : (kind + 1) * columns
            ]

    @pl.loop(0, GROUP // unroll)
    def _(step):
        for turn in range(unroll):
            one_pair(step * unroll + turn)

    begin = 0
    for out_ref in out_refs:
        count = out_ref.shape[0]
        for kind in range(4):
            values = rows_ref[kind, begin * GROUP : (begin + count) * GROUP, :]
            out_ref[:, kind] = values.reshape(count, GROUP, columns).astype(jnp.bfloat16)
        begin += count


def legendre_rows(m_of_pair, legendre, coef, row_of_slot, parts, first, groups, unroll):
    length, pairs_dev, heights = legendre.shape
    columns = coef.shape[2]
    slots = row_of_slot.shape[0]
    pairs = groups * GROUP
    return pl.pallas_call(
        functools.partial(
            legendre_kernel, length=length, first=first, pairs_dev=pairs_dev, unroll=unroll
        ),
        out_shape=[jax.ShapeDtypeStruct((part, 4, pairs, columns), jnp.bfloat16) for part in parts],
        grid_spec=pltpu.PrefetchScalarGridSpec(
            num_scalar_prefetch=1,
            grid=(groups,),
            in_specs=[
                pl.BlockSpec((slots,), lambda group, wave: (0,)),
                pl.BlockSpec((length, GROUP, heights), lambda group, wave: (0, first + group, 0)),
                pl.BlockSpec((length, GROUP, columns), lambda group, wave: (0, first + group, 0)),
            ],
            out_specs=[
                pl.BlockSpec((part, 4, GROUP, columns), lambda group, wave: (0, 0, group, 0))
                for part in parts
            ],
            scratch_shapes=[
                pltpu.VMEM((slots, heights), jnp.bfloat16),
                pltpu.VMEM((pl.cdiv(heights, LANES), length * GROUP, LANES), jnp.float32),
                pltpu.VMEM((length * GROUP, columns), jnp.float32),
                pltpu.VMEM((4, slots * GROUP, columns), jnp.float32),
            ],
        ),
        compiler_params=pltpu.CompilerParams(vmem_limit_bytes=56 << 20),
        cost_estimate=pl.CostEstimate(
            flops=2 * pairs * 4 * columns * heights * (length + slots),
            bytes_accessed=2 * pairs * (length * (heights + columns) + slots * 4 * columns),
            transcendentals=0,
        ),
    )(m_of_pair, row_of_slot, legendre, coef)


def legendre_rows_plain(low_m, row_of_slot, legendre, coef):
    length = legendre.shape[0]
    fields = coef.shape[2] // 2
    position = jnp.arange(length, dtype=jnp.int32)[:, None]
    cut = (length - 1 - low_m)[None, :]
    in_low = position < cut
    parity = jnp.where(in_low, position, position + cut) % 2
    sign = jnp.where(parity == 0, 1.0, -1.0).astype(jnp.bfloat16)[:, :, None]
    kinds = []
    for keep in (in_low, ~in_low):
        kept = jnp.where(keep[:, :, None], coef, jnp.zeros((), coef.dtype))
        for part in range(2):
            values = kept[:, :, part * fields : (part + 1) * fields]
            kinds.append(jnp.concatenate([values, values * sign], axis=2))
    fourier = jnp.einsum(
        "kph,kpqc->hqpc", legendre, jnp.stack(kinds, axis=2), preferred_element_type=jnp.float32
    ).astype(jnp.bfloat16)
    taken = jnp.take(fourier, jnp.maximum(row_of_slot, 0), axis=0)
    return jnp.where((row_of_slot >= 0)[:, None, None, None], taken, jnp.zeros((), taken.dtype))


def dft_kernel(rows_ref, table_ref, *refs):
    *others, out_ref = refs
    for slot in range(out_ref.shape[0]):
        rows = rows_ref[:, slot].reshape(table_ref.shape[0], rows_ref.shape[3])
        values = lax.dot_general(
            rows, table_ref[...], (((0,), (0,)), ((), ())), preferred_element_type=jnp.float32
        ).reshape(out_ref.shape[1:])
        if others:
            values = values + others[0][slot]
        out_ref[slot] = values.astype(out_ref.dtype)


def dft_rows(rows, table, begin, total, first, step, *others):
    sources, slots, depth, columns = rows.shape
    depth = depth * sources
    out_block = (step, 2, columns // 2, table.shape[1])
    out_spec = pl.BlockSpec(out_block, lambda block: (first // step + block, 0, 0, 0))
    return pl.pallas_call(
        dft_kernel,
        out_shape=jax.ShapeDtypeStruct(
            (total,) + out_block[1:], jnp.bfloat16 if others else jnp.float32
        ),
        grid=(pl.cdiv(slots, step),),
        in_specs=[
            pl.BlockSpec((sources, step) + rows.shape[2:], lambda block: (0, block, 0, 0)),
            pl.BlockSpec(
                (depth, table.shape[1]),
                lambda block: (begin // depth, 0),
                pipeline_mode=pl.Buffered(1),
            ),
        ]
        + [out_spec, pl.BlockSpec(memory_space=pl.ANY)][: len(others)],
        out_specs=out_spec,
        input_output_aliases={3: 0} if len(others) > 1 else {},
        compiler_params=pltpu.CompilerParams(vmem_limit_bytes=58 << 20),
        cost_estimate=pl.CostEstimate(
            flops=2 * slots * columns * depth * table.shape[1],
            bytes_accessed=2 * rows.size + (2 * depth + 6 * slots * columns) * table.shape[1],
            transcendentals=0,
        ),
    )(rows, table, *others)


def dft_rows_plain(rows, table):
    sources, slots, depth, columns = rows.shape
    values = jnp.einsum(
        "dlkc,dkj->lcj", rows, table.reshape(sources, depth, -1), preferred_element_type=jnp.float32
    )
    return values.astype(jnp.bfloat16).reshape(slots, 2, columns // 2, -1)


def dft_table(m_of_pair, wave_count, pairs_dev, cuts):
    low = m_of_pair.reshape(-1, 1, 1, pairs_dev)
    wave = jnp.concatenate([low, wave_count - 1 - low], axis=1)
    wave = jnp.broadcast_to(wave, (wave.shape[0], 2, 2, pairs_dev))
    shift = jnp.broadcast_to(jnp.array([0, NLON // 4], jnp.int32)[:, None], wave.shape)
    order = lambda values: jnp.concatenate(
        [values[..., begin:end].reshape(-1) for begin, end in cuts]
    )[:, None]
    wave, shift = order(wave), order(shift)
    longitude = jnp.arange(NLON, dtype=jnp.int32)
    angles = ((wave * longitude + shift) % NLON).astype(jnp.float32) * (2.0 * math.pi / NLON)
    weights = jnp.where(wave == 0, 1.0, 2.0).astype(jnp.float32)
    return (weights * jnp.cos(angles)).astype(jnp.bfloat16)


def dft_table_plain(m_of_pair, wave_count, pairs_dev):
    low = m_of_pair.reshape(-1, 1, pairs_dev)
    wave = jnp.concatenate([low, wave_count - 1 - low], axis=1)[..., None]
    longitude = jnp.arange(NLON, dtype=jnp.int32)
    angles = (wave * longitude % NLON).astype(jnp.float32) * (2.0 * math.pi / NLON)
    weights = jnp.where(wave == 0, 1.0, 2.0).astype(jnp.float32)
    table = jnp.stack([weights * jnp.cos(angles), -weights * jnp.sin(angles)], axis=2)
    return table.astype(jnp.bfloat16).reshape(-1, NLON)


def spectrum_terms(coef, low_m):
    pairs_dev, length, columns = coef.shape
    wave_count = length - 1
    fields = columns // 2
    squares = coef.astype(jnp.float32) ** 2
    power_sum = squares[:, :, :fields] + squares[:, :, fields:]
    padded = jnp.concatenate(
        [jnp.zeros((pairs_dev, wave_count, fields), jnp.float32), power_sum[:, :wave_count]], axis=1
    )
    shifted = jax.vmap(
        lambda values, offset: lax.dynamic_slice_in_dim(values, offset, wave_count, 0)
    )(padded, wave_count - low_m)
    degree = jnp.arange(wave_count, dtype=jnp.int32)
    high_keep = (degree[None, :] >= (wave_count - 1 - low_m)[:, None]).astype(jnp.float32)
    high_terms = power_sum[:, 1:] * high_keep[:, :, None]
    low_weight = jnp.where(low_m == 0, 1.0, 2.0).astype(jnp.float32)
    return jnp.sum(low_weight[:, None, None] * shifted + 2.0 * high_terms, axis=0)


def spectrum_kernel(wave_ref, coef_ref, after_ref, out_ref, coef32_ref, low_ref, high_ref, *, pairs_dev):
    group = pl.program_id(0)
    base = lax.axis_index("lat") * pairs_dev + group * GROUP
    length, _, columns = coef_ref.shape
    wave_count = length - 1

    @pl.when(group == 0)
    def _():
        low_ref[...] = jnp.zeros_like(low_ref)
        high_ref[...] = jnp.zeros_like(high_ref)

    coef32_ref[...] = coef_ref[...].astype(jnp.float32).reshape(coef32_ref.shape)
    position = lax.broadcasted_iota(jnp.int32, (length, columns), 0)

    @pl.loop(0, GROUP)
    def _(member):
        low = wave_ref[base + member]
        values = coef32_ref[pl.ds(member, length, stride=GROUP), :]
        power = values * values
        in_low = position < wave_count - low
        weight = jnp.where(low == 0, 1.0, 2.0)
        low_ref[pl.ds(low, length), :] += jnp.where(in_low, weight * power, 0.0)
        high_ref[...] += jnp.where(in_low, 0.0, 2.0 * power)

    @pl.when(group == pl.num_programs(0) - 1)
    def _():
        terms = low_ref[pl.ds(0, wave_count), :] + high_ref[pl.ds(1, wave_count), :]
        terms = terms + pltpu.roll(terms, columns // 2, 1)
        out_ref[...] = terms[:, : columns // 2]


def spectrum_sums(m_of_pair, coef, after):
    length, pairs_dev, columns = coef.shape
    spare = length + (m_of_pair.shape[0] + 7) // 8 * 8
    return pl.pallas_call(
        functools.partial(spectrum_kernel, pairs_dev=pairs_dev),
        out_shape=jax.ShapeDtypeStruct((length - 1, columns // 2), jnp.float32),
        grid_spec=pltpu.PrefetchScalarGridSpec(
            num_scalar_prefetch=1,
            grid=(pairs_dev // GROUP,),
            in_specs=[
                pl.BlockSpec((length, GROUP, columns), lambda group, wave: (0, group, 0)),
                pl.BlockSpec(memory_space=pl.ANY),
            ],
            out_specs=pl.BlockSpec((length - 1, columns // 2), lambda group, wave: (0, 0)),
            scratch_shapes=[
                pltpu.VMEM((length * GROUP, columns), jnp.float32),
                pltpu.VMEM((spare, columns), jnp.float32),
                pltpu.VMEM((length, columns), jnp.float32),
            ],
        ),
        compiler_params=pltpu.CompilerParams(vmem_limit_bytes=58 << 20),
        cost_estimate=pl.CostEstimate(
            flops=8 * coef.size, bytes_accessed=2 * coef.size, transcendentals=0
        ),
    )(m_of_pair, coef, after)


def sum_kernel(own_ref, *refs, scale):
    *got, _, out_ref = refs
    summed = own_ref[...]
    for piece in got:
        summed = summed + piece[...]
    if scale:
        first = lax.axis_index("lat") * own_ref.shape[0]
        degree = (first + lax.broadcasted_iota(jnp.int32, own_ref.shape, 0)).astype(jnp.float32)
        summed = summed * (scale / (2.0 * degree + 1.0))
    out_ref[...] = summed


def sum_pieces(pieces, after, scale=0):
    shape = pieces[0].shape
    whole = pl.BlockSpec(shape, lambda: (0, 0))
    return pl.pallas_call(
        functools.partial(sum_kernel, scale=scale),
        out_shape=jax.ShapeDtypeStruct(shape, pieces[0].dtype),
        in_specs=[whole] * len(pieces) + [pl.BlockSpec(memory_space=pl.ANY)],
        out_specs=whole,
        compiler_params=pltpu.CompilerParams(vmem_limit_bytes=58 << 20),
    )(*pieces, after)


def gate_kernel(*refs):
    pass


def gate(value, after):
    anywhere = pl.BlockSpec(memory_space=pl.ANY)
    return pl.pallas_call(
        gate_kernel,
        out_shape=jax.ShapeDtypeStruct(value.shape, value.dtype),
        in_specs=[anywhere, anywhere],
        out_specs=anywhere,
        input_output_aliases={0: 0},
        compiler_params=pltpu.CompilerParams(vmem_limit_bytes=58 << 20),
    )(value, after)


def scatter_round(terms, sources, stride, members):
    index = lax.axis_index("lat") // stride % members
    axis = 1 if stride == 1 and terms.ndim == 4 else 0
    mine = lambda step: lax.dynamic_index_in_dim(terms, index ^ step, axis, keepdims=False)
    pieces = [mine(0)]
    for step in range(1, members):
        pairs = [(i, i ^ (step * stride)) for i in range(sources)]
        pieces.append(lax.ppermute(mine(step), "lat", pairs))
    return [piece.reshape(-1, terms.shape[-1]) for piece in pieces]


def exchange(outgoing, sources):
    incoming = lax.all_to_all(
        outgoing.reshape(outgoing.shape[0], -1, outgoing.shape[3]), "lat", split_axis=0, concat_axis=0, tiled=True
    )
    return incoming.reshape((sources, -1) + incoming.shape[1:])


def local(coef, legendre, m_of_pair, row_of_slot):
    pairs_dev, length, columns = coef.shape
    wave_count = length - 1
    device = lax.axis_index("lat")
    sources = m_of_pair.shape[0] // pairs_dev
    low_m = lax.dynamic_slice_in_dim(m_of_pair, device * pairs_dev, pairs_dev)
    legend_rows = jnp.transpose(legendre, (1, 0, 2))
    coef_rows = jnp.transpose(coef, (1, 0, 2))
    if pairs_dev % GROUP == 0 and pairs_dev > GROUP and sources == 16 and row_of_slot.shape[0] % (sources * STEP):
        groups = pairs_dev // GROUP
        rest = pairs_dev - GROUP
        head = functools.partial(legendre_rows, m_of_pair, legend_rows, coef_rows)
        slots = row_of_slot.shape[0]
        slots_dev = slots // sources
        main = slots_dev - slots_dev % STEP
        (outgoing,) = head(row_of_slot, [slots], groups - 1, 1, 8)
        first_in = exchange(outgoing, sources)
        by_device = row_of_slot.reshape(sources, slots_dev)
        order = jnp.concatenate([by_device[:, :main].reshape(-1), by_device[:, main:].reshape(-1)])
        main_out, last_out = head(
            order, [sources * main, sources * (slots_dev - main)], 0, groups - 1, 2
        )
        main_in = exchange(main_out, sources)
        table = dft_table(m_of_pair, wave_count, pairs_dev, ((0, rest), (rest, pairs_dev)))
        partial = dft_rows(first_in, table, 4 * sources * rest, slots_dev, 0, STEP)
        grid_out = dft_rows(main_in, table, 0, slots_dev, 0, STEP, partial)
        terms = spectrum_sums(m_of_pair, coef_rows, outgoing)
        terms = terms.reshape(sources // 4, 4, -1, columns // 2)
        terms = sum_pieces(scatter_round(terms, sources, 1, 4), partial)
        terms = terms.reshape(sources // 4, -1, columns // 2)
        pieces = scatter_round(terms, sources, 4, sources // 4)
        last_in = exchange(gate(last_out, pieces[0]), sources)
        grid_out = dft_rows(last_in, table, 0, slots_dev, main, 1, partial, grid_out)
        spectrum = sum_pieces(pieces, grid_out, wave_count)
    else:
        outgoing = legendre_rows_plain(low_m, row_of_slot, legend_rows, coef_rows)
        table = dft_table_plain(m_of_pair, wave_count, pairs_dev)
        grid_out = dft_rows_plain(exchange(outgoing, sources), table)
        terms = spectrum_terms(coef, low_m)
        summed = lax.psum_scatter(terms, "lat", scatter_dimension=0, tiled=True)
        local_degree = (
            device * summed.shape[0] + jnp.arange(summed.shape[0], dtype=jnp.int32)
        ).astype(jnp.float32)
        spectrum = summed * (wave_count / (2.0 * local_degree + 1.0))[:, None]
    return (grid_out, spectrum)


def solution(mesh):
    in_specs = (P("lat", None, "slab"), P("lat", None, None), P(), P())
    out_specs = (P("lat", None, "slab", None), P("lat", "slab"))
    return jax.shard_map(local, mesh=mesh, in_specs=in_specs, out_specs=out_specs, check_vma=False)
```
